32 devices in a mesh: blk: 4 (over x, core), ulysses: 8 (over z, y).
Axes of the slice: x: 2, y: 2, z: 4, core: 2. Of those that a mesh axis runs over, the one named last changes fastest.
Arguments:
- query_rows: bfloat16 [32, 4096, 128], P(None, ('blk', 'ulysses')), may hold values from -160 to 160
- out_grad: bfloat16 [32, 4096, 128], P(None, ('blk', 'ulysses')), may hold values from -6 to 6
- key_rows: bfloat16 [32, 512, 128], P(None, 'blk'), may hold values from -6 to 6
- value_rows: bfloat16 [32, 512, 128], P(None, 'blk'), may hold values from -6 to 6
- routes: int32 [4, 4], replicated, may hold values from 0 to 7
Outputs:
- query_grad: bfloat16 [32, 4096, 128], P(None, ('blk', 'ulysses'))
- key_grad: float32 [32, 512, 128], P(None, ('blk', 'ulysses'))
- value_grad: float32 [32, 512, 128], P(None, ('blk', 'ulysses'))
The draws below stay inside these ranges and needn't reach their ends.
All inputs are finite; a program needn't handle non-finite values.
Results may differ from the reference program's by a relative error of at most 0.0056.
Values may be sent and summed in bfloat16 or wider, within the bound.
No kernel may reach another device: no remote copies, remote signals or barrier semaphores. Data moves between devices by JAX's collectives and lax.ppermute only.
A program may use at most 64 MiB of HBM per device.

```python
import math
import jax
import jax.numpy as jnp
from jax import lax

H = 32
HD = 128
TOK_DEV = 128
KB = 16
KBLOCKS = 8
KG = 128
QS = 1
TQB = 128
TOKENS = 4096
KEYS = 512
NK = 192
N_BLK = 4
N_ULYSSES = 8


def key_table(key):
    normal_draw = jax.random.truncated_normal(jax.random.fold_in(key, 11), -6.0, 6.0, (H, KEYS, HD), jnp.float32)
    return normal_draw


def draw_key_rows(key, part):
    normal_draw = key_table(key)
    return normal_draw.astype(jnp.bfloat16)


def draw_query_rows(key, part):
    normal_draw = jax.random.truncated_normal(jax.random.fold_in(key, 17), -6.0, 6.0, (H, TOKENS, HD), jnp.float32)
    return normal_draw.astype(jnp.bfloat16)


def place_ends(values, stream_key, smallest, largest):
    index_at = [jax.random.randint(jax.random.fold_in(stream_key, axis), (), 0, length) for axis, length in enumerate(values.shape)]
    main_axis = values.shape.index(max(values.shape))
    next_to = index_at[:main_axis] + [(index_at[main_axis] + 1) % values.shape[main_axis]] + index_at[main_axis + 1:]
    return values.at[tuple(index_at)].set(smallest).at[tuple(next_to)].set(largest)


def block_levels(own_key, extent, shards, smallest, largest):
    level = 1.0
    for dim, shards_of in shards:
        draws = jax.random.uniform(jax.random.fold_in(jax.random.fold_in(own_key, 6), dim), (shards_of,), jnp.float32, smallest / len(shards), largest / len(shards))
        level = level * jnp.repeat(jnp.exp(draws), extent[dim] // shards_of).reshape((-1,) + (1,) * (len(extent) - 1 - dim))
    return level


def scatter_about(own_key, dims, scale, most, cuts=(), kind=jnp.bfloat16):
    values = jax.random.normal(own_key, dims, jnp.float32) * scale
    if len(cuts) > 0:
        values = block_levels(own_key, dims, cuts, -0.22, 0.18) * values
    return jnp.clip(values, min=-most, max=most).astype(kind)


def setup_inputs(seed: int = 0) -> dict:
    splits = jax.random.split(jax.random.key(seed), 6)
    query_rows = draw_query_rows(jax.random.fold_in(splits[5], 71), 0)
    out_grad = scatter_about(splits[1], (H, TOKENS, HD), 1.0, 6.0, ((1, 32),))
    key_rows = draw_key_rows(jax.random.fold_in(splits[5], 71), 0)
    value_rows = scatter_about(splits[3], (H, KEYS, HD), 1.0, 6.0, ((1, 4),))
    routes = place_ends(jax.random.randint(splits[4], (N_BLK, N_BLK), 0, KBLOCKS), jax.random.fold_in(splits[4], 1), 0, KBLOCKS - 1).astype(jnp.int32)
    return {"query_rows": query_rows, "out_grad": out_grad, "key_rows": key_rows, "value_rows": value_rows, "routes": routes}


def reference(query_rows, out_grad, key_rows, value_rows, routes):
    group_length = TOK_DEV * N_ULYSSES
    key_stride = group_length // KG
    score_scale = 1.0 / math.sqrt(HD)
    group_ids = jnp.arange(N_BLK, dtype=jnp.int32)
    block_offsets = jnp.arange(KB, dtype=jnp.int32)
    own_offsets = jnp.arange(KG, dtype=jnp.int32)
    positions = jnp.arange(group_length, dtype=jnp.int32)

    def one_group(totals, group_index):
        key_total, value_total = totals
        queries = lax.dynamic_slice_in_dim(query_rows, group_index * group_length, group_length, 1).astype(jnp.float32)
        grad_rows = lax.dynamic_slice_in_dim(out_grad, group_index * group_length, group_length, 1).astype(jnp.float32)
        chosen = lax.dynamic_index_in_dim(routes, group_index, 0, keepdims=False).astype(jnp.int32)
        routed_ids = (group_ids[:, None] * KG + chosen[:, None] * KB + block_offsets[None, :]).reshape(-1)
        key_ids = jnp.concatenate([group_index * KG + own_offsets, routed_ids]).astype(jnp.int32)
        near_keys = jnp.take(key_rows, key_ids, axis=1).astype(jnp.float32)
        near_values = jnp.take(value_rows, key_ids, axis=1).astype(jnp.float32)
        own_visible = own_offsets[None, :] * key_stride <= positions[:, None]
        far_visible = jnp.broadcast_to(jnp.repeat(group_ids < group_index, KB)[None, :], (group_length, N_BLK * KB))
        visible = jnp.concatenate([own_visible, far_visible], axis=1)[None]
        scores = jnp.einsum('htd,hkd->htk', queries, near_keys) * score_scale
        row_max = lax.optimization_barrier(jnp.max(jnp.where(visible, scores, -jnp.inf), axis=-1, keepdims=True))
        expsum = jnp.where(visible, jnp.exp(scores - row_max), 0.0)
        weights = expsum / lax.optimization_barrier(jnp.sum(expsum, axis=-1, keepdims=True))
        weights_half = lax.optimization_barrier(weights.astype(jnp.bfloat16)).astype(jnp.float32)
        attended = jnp.einsum('htk,hkd->htd', weights_half, near_values)
        delta_rows = lax.optimization_barrier(jnp.sum(grad_rows * attended, axis=-1, keepdims=True))
        dweights = jnp.einsum('htd,hkd->htk', grad_rows, near_values)
        dscore = lax.optimization_barrier((weights * (dweights - delta_rows)).astype(jnp.bfloat16)).astype(jnp.float32)
        query_part = (jnp.einsum('htk,hkd->htd', dscore, near_keys) * score_scale).astype(jnp.bfloat16)
        split_score = dscore.reshape(H, N_ULYSSES, QS, TQB, NK)
        split_weight = weights_half.reshape(H, N_ULYSSES, QS, TQB, NK)
        split_query = queries.reshape(H, N_ULYSSES, QS, TQB, HD)
        split_grad = grad_rows.reshape(H, N_ULYSSES, QS, TQB, HD)
        key_part = jnp.einsum('husrk,husrd->shkd', split_score, split_query) * score_scale
        value_part = jnp.einsum('husrk,husrd->shkd', split_weight, split_grad)
        key_total = key_total.at[:, :, key_ids, :].add(key_part)
        value_total = value_total.at[:, :, key_ids, :].add(value_part)
        return ((key_total, value_total), query_part)
    zeros_total = jnp.zeros((QS, H, KEYS, HD), jnp.float32)
    (key_total, value_total), query_parts = lax.scan(one_group, (zeros_total, zeros_total), group_ids)
    query_grad = jnp.moveaxis(query_parts, 0, 1).reshape(H, TOKENS, HD)
    key_grad = lax.optimization_barrier(jnp.sum(lax.optimization_barrier(key_total.astype(jnp.bfloat16)).astype(jnp.float32), axis=0))
    value_grad = lax.optimization_barrier(jnp.sum(lax.optimization_barrier(value_total.astype(jnp.bfloat16)).astype(jnp.float32), axis=0))
    return (query_grad, key_grad, value_grad)
```

```python
import functools
import math

import jax
import jax.numpy as jnp
from jax import lax
from jax.experimental import pallas as pl
from jax.experimental.pallas import tpu as pltpu
from jax.sharding import PartitionSpec as P

KB = 16
CHUNKS = 1


def attend_kernel(far_slots, place, query, grad, keys, values, *rest):
    far_rows = rest[:far_slots]
    query_out, own_out = rest[-2 - far_slots :][:2]
    far_outs = rest[len(rest) - far_slots :]
    heads, tokens, head_dim = query.shape
    group_keys = keys.shape[1]
    group, first_token, key_stride = place[0], place[1], place[2]
    score_scale = 1.0 / math.sqrt(head_dim)
    exp_scale = score_scale * math.log2(math.e)
    key_at = lax.broadcasted_iota(jnp.int32, (group_keys, tokens), 0) * key_stride
    token_at = lax.broadcasted_iota(jnp.int32, (group_keys, tokens), 1) + first_token
    own_hidden = jnp.where(key_at <= token_at, 0.0, -jnp.inf)
    hidden = [own_hidden]
    for slot in range(far_slots):
        seen = jnp.where(group >= slot + 1, 0.0, -jnp.inf)
        hidden.append(jnp.full((KB, tokens), seen, jnp.float32))
    hidden = jnp.concatenate(hidden, axis=0)
    nt = (((1,), (1,)), ((), ()))
    tn = (((0,), (0,)), ((), ()))
    for head in range(heads):
        q = query[head]
        g = grad[head]
        near_keys = jnp.concatenate([keys[head]] + [f[0, head] for f in far_rows], axis=0)
        near_values = jnp.concatenate([values[head]] + [f[1, head] for f in far_rows], axis=0)
        scores = lax.dot_general(near_keys, q, nt, preferred_element_type=jnp.float32) + hidden
        dweights = lax.dot_general(near_values, g, nt, preferred_element_type=jnp.float32)
        row_max = jnp.max(scores, axis=0, keepdims=True)
        expsum = jnp.exp2((scores - row_max) * exp_scale)
        weights = expsum * (1.0 / jnp.sum(expsum, axis=0, keepdims=True))
        weights_half = weights.astype(jnp.bfloat16)
        delta = jnp.sum(weights_half.astype(jnp.float32) * dweights, axis=0, keepdims=True)
        dscore = (weights * (dweights - delta)).astype(jnp.bfloat16)
        query_grad = lax.dot_general(dscore, near_keys, tn, preferred_element_type=jnp.float32)
        query_out[head] = (query_grad * score_scale).astype(jnp.bfloat16)
        key_part = jnp.dot(dscore, q, preferred_element_type=jnp.float32) * score_scale
        value_part = jnp.dot(weights_half, g, preferred_element_type=jnp.float32)
        key_part = key_part.astype(jnp.bfloat16)
        value_part = value_part.astype(jnp.bfloat16)
        own_out[0, head] = key_part[:group_keys]
        own_out[1, head] = value_part[:group_keys]
        for slot, far_out in enumerate(far_outs):
            rows = slice(group_keys + slot * KB, group_keys + (slot + 1) * KB)
            far_out[0, head] = key_part[rows]
            far_out[1, head] = value_part[rows]


def attend(place, query, grad, keys, values, far, first_head, chunk_heads, query_out):
    head_count, tokens, head_dim = query.shape
    group_keys = keys.shape[1]
    step_heads = math.gcd(4, chunk_heads)
    first_step = first_head // step_heads

    def rows(count):
        return pl.BlockSpec((step_heads, count, head_dim), lambda i, place: (i + first_step, 0, 0))

    def pair(count):
        return pl.BlockSpec((2, step_heads, count, head_dim), lambda i, place: (0, i, 0, 0))

    operands = [place, query, grad, keys, values, *far]
    in_specs = [rows(tokens), rows(tokens), rows(group_keys), rows(group_keys)]
    in_specs += [pair(KB)] * len(far)
    aliases = {}
    if query_out is not None:
        aliases = {len(operands): 0}
        operands.append(query_out)
        in_specs.append(pl.BlockSpec(memory_space=pl.ANY))
    outs = pl.pallas_call(
        functools.partial(attend_kernel, len(far)),
        out_shape=[
            jax.ShapeDtypeStruct(query.shape, jnp.bfloat16),
            jax.ShapeDtypeStruct((2, chunk_heads, group_keys, head_dim), jnp.bfloat16),
        ]
        + [jax.ShapeDtypeStruct((2, chunk_heads, KB, head_dim), jnp.bfloat16)] * len(far),
        grid_spec=pltpu.PrefetchScalarGridSpec(
            num_scalar_prefetch=1,
            grid=(chunk_heads // step_heads,),
            in_specs=in_specs,
            out_specs=[rows(tokens), pair(group_keys)] + [pair(KB)] * len(far),
        ),
        input_output_aliases=aliases,
        name="attend",
    )(*operands)
    return outs[0], outs[1], outs[2:]


def swap_pairs(size, bit):
    return [(rank, rank ^ bit) for rank in range(size)]


def body(query_rows, out_grad, key_rows, value_rows, routes):
    head_count, token_count, head_dim = query_rows.shape
    group_keys = key_rows.shape[1]
    groups = lax.axis_size("blk")
    ranks = lax.axis_size("ulysses")
    my_group = lax.axis_index("blk")
    my_rank = lax.axis_index("ulysses")
    block_count = group_keys // KB
    key_stride = token_count * ranks // group_keys
    rank_keys = group_keys // ranks
    place = jnp.stack([my_group, my_rank * token_count, jnp.int32(key_stride)]).astype(jnp.int32)
    chunk_heads = head_count // CHUNKS
    bits = [1 << b for b in range(ranks.bit_length() - 1)]
    orders = [bits]

    def route(asker, holder):
        return routes[jnp.clip(asker, 0, groups - 1), jnp.clip(holder, 0, groups - 1)]

    key_blocks = key_rows.reshape(head_count, block_count, KB, head_dim)
    value_blocks = value_rows.reshape(head_count, block_count, KB, head_dim)

    def routed(first_head, distance):
        block = route(my_group + distance, my_group)
        picked = [
            lax.dynamic_slice(
                rows, (first_head, block, 0, 0), (chunk_heads, 1, KB, head_dim)
            ).reshape(chunk_heads, KB, head_dim)
            for rows in (key_blocks, value_blocks)
        ]
        pairs = [(g, g + distance) for g in range(groups - distance)]
        return lax.ppermute(jnp.stack(picked), "blk", pairs)

    def send_back(part, distance):
        pairs = [(g + distance, g) for g in range(groups - distance)]
        return lax.ppermute(part, "blk", pairs)

    def add_back(own, back):
        total = own.reshape(2, chunk_heads, block_count, KB, head_dim).astype(jnp.float32)
        block_ids = jnp.arange(block_count, dtype=jnp.int32)[None, None, :, None, None]
        for distance, part in enumerate(back, 1):
            block = route(my_group + distance, my_group)
            total = total + jnp.where(
                block_ids == block, part[:, :, None].astype(jnp.float32), 0.0
            )
        return total.astype(jnp.bfloat16)

    def scatter(total, order):
        shape = (2, chunk_heads) + (2,) * len(bits) + (rank_keys, head_dim)
        total = total.reshape(shape)
        left = list(reversed(bits))
        for bit in order:
            axis = 2 + left.index(bit)
            mine = (my_rank // bit) % 2
            sent = lax.dynamic_index_in_dim(total, 1 - mine, axis, keepdims=False)
            kept = lax.dynamic_index_in_dim(total, mine, axis, keepdims=False)
            came = lax.ppermute(sent, "ulysses", swap_pairs(ranks, bit))
            left.remove(bit)
            total = kept.astype(jnp.float32) + came.astype(jnp.float32)
            if left:
                total = total.astype(jnp.bfloat16)
        return total

    far = [
        [routed(chunk * chunk_heads, d) for d in range(1, groups)] for chunk in range(CHUNKS)
    ]
    query_out = None
    results = []
    for chunk in range(CHUNKS):
        query_out, own, parts = attend(
            place, query_rows, out_grad, key_rows, value_rows, far[chunk],
            chunk * chunk_heads, chunk_heads, query_out,
        )
        back = [send_back(part, d) for d, part in enumerate(parts, 1)]
        results.append(scatter(add_back(own, back), orders[chunk % len(orders)]))
    key_grad = jnp.concatenate([r[0] for r in results], axis=0)
    value_grad = jnp.concatenate([r[1] for r in results], axis=0)
    return (query_out, key_grad, value_grad)


def solution(mesh):
    return jax.shard_map(
        body,
        mesh=mesh,
        in_specs=(
            P(None, ("blk", "ulysses"), None),
            P(None, ("blk", "ulysses"), None),
            P(None, "blk", None),
            P(None, "blk", None),
            P(),
        ),
        out_specs=(
            P(None, ("blk", "ulysses"), None),
            P(None, ("blk", "ulysses"), None),
            P(None, ("blk", "ulysses"), None),
        ),
        check_vma=False,
    )
```

```python
import functools
import math

import jax
import jax.numpy as jnp
from jax import lax
from jax.experimental import pallas as pl
from jax.experimental.pallas import tpu as pltpu
from jax.sharding import PartitionSpec as P

KB = 16
CHUNKS = 2
STEP_HEADS = 8
VMEM_SMALL = 8 << 20
VMEM_ATTEND = 24 << 20


def far_masks(groups):
    return [1] + [mask for even in range(2, groups, 2) for mask in (even, even ^ 1)]


def pick_kernel(cuts, groups, routes, keys, values, *rest):
    outs, arrived = rest[:-1], rest[-1]
    group = lax.axis_index("blk")
    copies = []
    for cut, (first_head, heads) in enumerate(cuts):
        for index, mask in enumerate(far_masks(groups)):
            out = outs[cut * (groups // 2) + (index + 1) // 2]
            out = out if index == 0 else out.at[(index + 1) % 2]
            start = pl.multiple_of(routes[group ^ mask, group] * KB, KB)
            for side, rows in enumerate((keys, values)):
                copies.append(
                    pltpu.make_async_copy(
                        rows.at[pl.ds(first_head, heads), pl.ds(start, KB)],
                        out.at[side],
                        arrived.at[cut, index, side],
                    )
                )
    for copy in copies:
        copy.start()
    for copy in copies:
        copy.wait()


def pick(routes, keys, values, groups, cuts):
    head_dim = keys.shape[2]
    shapes = []
    for _, heads in cuts:
        block = (2, heads, KB, head_dim)
        shapes += [block] + [(2,) + block] * (groups // 2 - 1)
    outs = pl.pallas_call(
        functools.partial(pick_kernel, cuts, groups),
        out_shape=[jax.ShapeDtypeStruct(shape, jnp.bfloat16) for shape in shapes],
        in_specs=[pl.BlockSpec(memory_space=pltpu.SMEM)]
        + [pl.BlockSpec(memory_space=pltpu.HBM)] * 2,
        out_specs=[pl.BlockSpec(memory_space=pltpu.VMEM)] * len(shapes),
        scratch_shapes=[pltpu.SemaphoreType.DMA((len(cuts), groups - 1, 2))],
        compiler_params=pltpu.CompilerParams(vmem_limit_bytes=VMEM_SMALL),
        name="pick",
    )(routes, keys, values)
    per_cut = groups // 2
    return [outs[i * per_cut : (i + 1) * per_cut] for i in range(len(cuts))]


def slot_specs(groups, step_heads, rows, head_dim):
    flat = pl.BlockSpec((2, step_heads) + rows + (head_dim,), lambda i: (0, i) + (0,) * (len(rows) + 1))
    half = pl.BlockSpec(
        (None, 2, step_heads) + rows + (head_dim,), lambda i: (0, 0, i) + (0,) * (len(rows) + 1)
    )
    return [flat] + [half, flat] * (groups // 2 - 1)


def attend_kernel(masks, has_alias, query, grad, keys, values, *rest):
    slots = len(masks)
    far_rows = rest[:slots]
    rest = rest[slots + has_alias :]
    query_out, own_out, near_out = rest[:3]
    pair_outs = rest[3 : 3 + slots // 2]
    far_outs = [near_out] + [out.at[half] for out in pair_outs for half in range(2)]
    score_ref, dweight_ref, half_ref, dscore_ref = rest[3 + slots // 2 :]
    heads, tokens, head_dim = query.shape
    group_keys = keys.shape[1]
    group = lax.axis_index("blk")
    rank = lax.axis_index("ulysses")
    key_stride = tokens * lax.axis_size("ulysses") // group_keys
    score_scale = 1.0 / math.sqrt(head_dim)
    exp_scale = score_scale * math.log2(math.e)
    key_at = lax.broadcasted_iota(jnp.int32, (group_keys, tokens), 0) * key_stride
    token_at = lax.broadcasted_iota(jnp.int32, (group_keys, tokens), 1) + rank * tokens
    hidden = [jnp.where(key_at <= token_at, 0.0, -jnp.inf)]
    for mask in masks:
        seen = jnp.where((group ^ mask) < group, 0.0, -jnp.inf)
        hidden.append(jnp.full((KB, tokens), seen, jnp.float32))
    hidden = jnp.concatenate(hidden, axis=0)
    nt = (((1,), (1,)), ((), ()))
    tn = (((0,), (0,)), ((), ()))

    def near(rows, side, head):
        return jnp.concatenate([rows[head]] + [far[side, head] for far in far_rows], axis=0)

    for head in range(heads):
        score_ref[head] = lax.dot_general(
            near(keys, 0, head), query[head], nt, preferred_element_type=jnp.float32
        )
        dweight_ref[head] = lax.dot_general(
            near(values, 1, head), grad[head], nt, preferred_element_type=jnp.float32
        )
    for head in range(heads):
        scores = score_ref[head] + hidden
        dweights = dweight_ref[head]
        row_max = jnp.max(scores, axis=0, keepdims=True)
        expsum = jnp.exp2((scores - row_max) * exp_scale)
        weights = expsum * (1.0 / jnp.sum(expsum, axis=0, keepdims=True))
        weights_half = weights.astype(jnp.bfloat16)
        delta = jnp.sum(weights_half.astype(jnp.float32) * dweights, axis=0, keepdims=True)
        half_ref[head] = weights_half
        dscore_ref[head] = (weights * (dweights - delta)).astype(jnp.bfloat16)
    for head in range(heads):
        dscore = dscore_ref[head]
        query_grad = lax.dot_general(
            dscore, near(keys, 0, head), tn, preferred_element_type=jnp.float32
        )
        query_out[head] = (query_grad * score_scale).astype(jnp.bfloat16)
        key_part = jnp.dot(dscore, query[head], preferred_element_type=jnp.float32)
        value_part = jnp.dot(half_ref[head], grad[head], preferred_element_type=jnp.float32)
        parts = ((key_part * score_scale).astype(jnp.bfloat16), value_part.astype(jnp.bfloat16))
        for side, part in enumerate(parts):
            own_out[side, head] = part[:group_keys]
            for slot, far_out in enumerate(far_outs):
                start = group_keys + slot * KB
                far_out[side, head] = part[start : start + KB]


def attend(query, grad, keys, values, far, groups, first_head, chunk_heads, query_out):
    head_count, tokens, head_dim = query.shape
    group_keys = keys.shape[1]
    masks = far_masks(groups)
    near_keys = group_keys + KB * len(masks)
    step_heads = math.gcd(STEP_HEADS, math.gcd(chunk_heads, first_head))
    first_step = first_head // step_heads

    def rows(count):
        return pl.BlockSpec((step_heads, count, head_dim), lambda i: (i + first_step, 0, 0))

    def pair(count):
        return pl.BlockSpec((2, step_heads, count, head_dim), lambda i: (0, i, 0, 0))

    both = pl.BlockSpec((2, 2, step_heads, KB, head_dim), lambda i: (0, 0, i, 0, 0))
    operands = [query, grad, keys, values, *far]
    in_specs = [rows(tokens), rows(tokens), rows(group_keys), rows(group_keys)]
    in_specs += slot_specs(groups, step_heads, (KB,), head_dim)
    aliases = {}
    if query_out is not None:
        aliases = {len(operands): 0}
        operands.append(query_out)
        in_specs.append(pl.BlockSpec(memory_space=pl.ANY))
    block = (2, chunk_heads, KB, head_dim)
    shapes = [query.shape, (2, chunk_heads, group_keys, head_dim), block]
    shapes += [(2,) + block] * (groups // 2 - 1)
    outs = pl.pallas_call(
        functools.partial(attend_kernel, masks, query_out is not None),
        out_shape=[jax.ShapeDtypeStruct(shape, jnp.bfloat16) for shape in shapes],
        grid=(chunk_heads // step_heads,),
        in_specs=in_specs,
        out_specs=[rows(tokens), pair(group_keys), pair(KB)] + [both] * (groups // 2 - 1),
        scratch_shapes=[pltpu.VMEM((step_heads, near_keys, tokens), jnp.float32)] * 2
        + [pltpu.VMEM((step_heads, near_keys, tokens), jnp.bfloat16)] * 2,
        input_output_aliases=aliases,
        compiler_params=pltpu.CompilerParams(vmem_limit_bytes=VMEM_ATTEND),
        name="attend",
    )(*operands)
    return outs[0], outs[1], outs[2:]


def merge_kernel(masks, bit, routes, own, *rest):
    slots = len(masks)
    back = rest[:slots]
    sent, kept, total = rest[slots:]
    group = lax.axis_index("blk")
    mine = (lax.axis_index("ulysses") // bit) % 2
    per_block = back[0].shape[2]
    total[...] = own[...].astype(jnp.float32)
    for mask, part in zip(masks, back):
        first = routes[group ^ mask, group] * per_block
        spot = pl.ds(first, per_block)
        total[:, :, spot] = total[:, :, spot] + part[...].astype(jnp.float32)
    for index in range(sent.shape[2]):
        base = index // bit * 2 * bit + index % bit
        for out, side in ((sent, 1 - mine), (kept, mine)):
            out[:, :, index] = total[:, :, base + side * bit].astype(jnp.bfloat16)


def merge(routes, own, back, groups, ranks, bit):
    _, chunk_heads, group_keys, head_dim = own.shape
    rank_keys = group_keys // ranks
    step_heads = math.gcd(STEP_HEADS, chunk_heads)
    masks = far_masks(groups)
    rows = (KB // rank_keys, rank_keys)

    def blocks(count):
        return pl.BlockSpec(
            (2, step_heads, count, rank_keys, head_dim), lambda i: (0, i, 0, 0, 0)
        )

    half = jax.ShapeDtypeStruct((2, chunk_heads, ranks // 2, rank_keys, head_dim), jnp.bfloat16)
    return pl.pallas_call(
        functools.partial(merge_kernel, masks, bit),
        out_shape=[half, half],
        grid=(chunk_heads // step_heads,),
        in_specs=[pl.BlockSpec(memory_space=pltpu.SMEM), blocks(ranks)]
        + slot_specs(groups, step_heads, rows, head_dim),
        out_specs=[blocks(ranks // 2)] * 2,
        scratch_shapes=[
            pltpu.VMEM((2, step_heads, ranks, rank_keys, head_dim), jnp.float32)
        ],
        compiler_params=pltpu.CompilerParams(vmem_limit_bytes=VMEM_ATTEND),
        name="merge",
    )(
        routes,
        own.reshape(2, chunk_heads, ranks, rank_keys, head_dim),
        *(part.reshape(part.shape[:-2] + rows + (head_dim,)) for part in back),
    )


def body(query_rows, out_grad, key_rows, value_rows, routes):
    head_count, token_count, head_dim = query_rows.shape
    query_rows, out_grad, key_rows, value_rows = (
        pltpu.with_memory_space_constraint(rows, pltpu.HBM)
        for rows in (query_rows, out_grad, key_rows, value_rows)
    )
    group_keys = key_rows.shape[1]
    groups = lax.axis_size("blk")
    ranks = lax.axis_size("ulysses")
    my_rank = lax.axis_index("ulysses")
    rank_keys = group_keys // ranks
    chunk_heads = head_count // CHUNKS
    cuts = [(chunk * chunk_heads, chunk_heads) for chunk in range(CHUNKS)]
    bits = [1 << b for b in range(ranks.bit_length() - 1)]
    orders = [bits, [bits[1], bits[0]] + bits[2:]]

    def exchange(near, pairs, forward):
        def hop(rows, mask, both=False):
            links = [
                (g, g ^ mask) for g in range(groups) if both or ((g ^ mask) > g) == forward
            ]
            return lax.ppermute(rows, "blk", links)

        crossed = [hop(pair, 2 * i) for i, pair in enumerate(pairs, 1)]
        slots = [hop(near, 1)]
        for pair in crossed:
            slots += [pair, hop(pair[1], 1, both=True)]
        return slots

    def scatter(sent, kept, order):
        left = [bit for bit in reversed(bits)]
        for step, bit in enumerate(order):
            left.remove(bit)
            if step:
                axis = 2 + sum(b > bit for b in left)
                mine = (my_rank // bit) % 2
                sent = lax.dynamic_index_in_dim(total, 1 - mine, axis, keepdims=False)
                kept = lax.dynamic_index_in_dim(total, mine, axis, keepdims=False)
            came = lax.ppermute(sent, "ulysses", [(r, r ^ bit) for r in range(ranks)])
            total = kept.astype(jnp.float32) + came.astype(jnp.float32)
            total = total.reshape(kept.shape[:2] + (2,) * len(left) + (rank_keys, head_dim))
            if left:
                total = total.astype(jnp.bfloat16)
        return total

    picked = pick(routes, key_rows, value_rows, groups, cuts)
    far = [exchange(parts[0], parts[1:], True) for parts in picked]
    query_out = None
    results = []
    for chunk, (first_head, heads) in enumerate(cuts):
        query_out, own, parts = attend(
            query_rows, out_grad, key_rows, value_rows, far[chunk], groups,
            first_head, heads, query_out,
        )
        back = exchange(parts[0], parts[1:], False)
        order = orders[chunk % len(orders)]
        sent, kept = merge(routes, own, back, groups, ranks, order[0])
        results.append(scatter(sent, kept, order))
    key_grad = jnp.concatenate([r[0] for r in results], axis=0)
    value_grad = jnp.concatenate([r[1] for r in results], axis=0)
    return (query_out, key_grad, value_grad)


def solution(mesh):
    return jax.shard_map(
        body,
        mesh=mesh,
        in_specs=(
            P(None, ("blk", "ulysses"), None),
            P(None, ("blk", "ulysses"), None),
            P(None, "blk", None),
            P(None, "blk", None),
            P(),
        ),
        out_specs=(
            P(None, ("blk", "ulysses"), None),
            P(None, ("blk", "ulysses"), None),
            P(None, ("blk", "ulysses"), None),
        ),
        check_vma=False,
    )
```

```python
import functools
import math

import jax
import jax.numpy as jnp
from jax import lax
from jax.experimental import pallas as pl
from jax.experimental.pallas import tpu as pltpu
from jax.sharding import PartitionSpec as P


KB = 16
PLAN = ((20, 12, False, 0), (0, 20, True, 0))
STEP_HEADS = 10
VMEM_SMALL = 8 << 20
VMEM_ATTEND = 24 << 20


def far_masks(groups):
    return [1] + [mask for even in range(2, groups, 2) for mask in (even, even ^ 1)]


def pick_kernel(cuts, groups, routes, query, grad, keys, values, *rest):
    outs, arrived = list(rest[:-1]), rest[-1]
    group = lax.axis_index("blk")
    half = lax.axis_index("ulysses") % 2
    copies = []
    for number, (first_head, heads, paired, _) in enumerate(cuts):
        if paired:
            heads //= 2
            other = first_head + (1 - half) * heads
            first_head = first_head + half * heads
            swapped = outs.pop(0)
            for side, rows in enumerate((query, grad)):
                copies.append(
                    pltpu.make_async_copy(
                        rows.at[pl.ds(other, heads)],
                        swapped.at[side],
                        arrived.at[number, groups - 1, side],
                    )
                )
        for index, mask in enumerate(far_masks(groups)):
            out = outs[(index + 1) // 2]
            out = out if index == 0 else out.at[(index + 1) % 2]
            start = pl.multiple_of(routes[group ^ mask, group] * KB, KB)
            for side, rows in enumerate((keys, values)):
                copies.append(
                    pltpu.make_async_copy(
                        rows.at[pl.ds(first_head, heads), pl.ds(start, KB)],
                        out.at[side],
                        arrived.at[number, index, side],
                    )
                )
        outs = outs[groups // 2 :]
    for copy in copies:
        copy.start()
    for copy in copies:
        copy.wait()


def pick(routes, query, grad, keys, values, groups, cuts):
    _, tokens, head_dim = query.shape
    shapes, counts = [], []
    for _, heads, paired, _ in cuts:
        heads = heads // 2 if paired else heads
        block = (2, heads, KB, head_dim)
        swap = [(2, heads, tokens, head_dim)] if paired else []
        shapes += swap + [block] + [(2,) + block] * (groups // 2 - 1)
        counts.append(len(swap) + groups // 2)
    outs = pl.pallas_call(
        functools.partial(pick_kernel, cuts, groups),
        out_shape=[jax.ShapeDtypeStruct(shape, jnp.bfloat16) for shape in shapes],
        in_specs=[pl.BlockSpec(memory_space=pltpu.SMEM)]
        + [pl.BlockSpec(memory_space=pltpu.HBM)] * 4,
        out_specs=[pl.BlockSpec(memory_space=pltpu.VMEM)] * len(shapes),
        scratch_shapes=[pltpu.SemaphoreType.DMA((len(cuts), groups, 2))],
        compiler_params=pltpu.CompilerParams(vmem_limit_bytes=VMEM_SMALL),
        name="pick",
    )(routes, query, grad, keys, values)
    picked = []
    for count, cut in zip(counts, cuts):
        mine, outs = outs[:count], outs[count:]
        picked.append((mine[0], mine[1:]) if cut[2] else (None, mine))
    return picked


def slot_specs(groups, step_heads, rows, head_dim):
    flat = pl.BlockSpec((2, step_heads) + rows + (head_dim,), lambda i, *_: (0, i) + (0,) * (len(rows) + 1))
    half = pl.BlockSpec(
        (None, 2, step_heads) + rows + (head_dim,), lambda i, *_: (0, 0, i) + (0,) * (len(rows) + 1)
    )
    return [flat] + [half, flat] * (groups // 2 - 1)


def attend_kernel(masks, has_alias, paired, _, query, grad, keys, values, *rest):
    slots = len(masks)
    far_rows = rest[:slots]
    swapped = rest[slots] if paired else None
    rest = rest[slots + has_alias + paired :]
    if paired:
        other_out, rest = rest[0], rest[1:]
    query_out, own_out, near_out = rest[:3]
    pair_outs = rest[3 : 3 + slots // 2]
    far_outs = [near_out] + [out.at[half] for out in pair_outs for half in range(2)]
    score_ref, dweight_ref, half_ref, dscore_ref = rest[3 + slots // 2 :]
    heads, tokens, head_dim = query.shape
    group_keys = keys.shape[1]
    group = lax.axis_index("blk")
    rank = lax.axis_index("ulysses")
    key_stride = tokens * lax.axis_size("ulysses") // group_keys
    score_scale = 1.0 / math.sqrt(head_dim)
    exp_scale = score_scale * math.log2(math.e)
    key_at = lax.broadcasted_iota(jnp.int32, (group_keys, tokens), 0) * key_stride
    token_at = lax.broadcasted_iota(jnp.int32, (group_keys, tokens), 1)
    sources = (rank, rank ^ 1) if paired else (rank,)
    hidden = [
        jnp.concatenate(
            [jnp.where(key_at <= token_at + source * tokens, 0.0, -jnp.inf) for source in sources],
            axis=1,
        )
    ]
    for mask in masks:
        seen = jnp.where((group ^ mask) < group, 0.0, -jnp.inf)
        hidden.append(jnp.full((KB, tokens * len(sources)), seen, jnp.float32))
    hidden = jnp.concatenate(hidden, axis=0)
    nt = (((1,), (1,)), ((), ()))
    tn = (((0,), (0,)), ((), ()))

    def near(rows, side, head):
        return jnp.concatenate([rows[head]] + [far[side, head] for far in far_rows], axis=0)

    def both(rows, side, head):
        if not paired:
            return rows[head]
        return jnp.concatenate([rows[head], swapped[side, head]], axis=0)

    for head in range(heads):
        score_ref[head] = lax.dot_general(
            near(keys, 0, head), both(query, 0, head), nt, preferred_element_type=jnp.float32
        )
        dweight_ref[head] = lax.dot_general(
            near(values, 1, head), both(grad, 1, head), nt, preferred_element_type=jnp.float32
        )
    for head in range(heads):
        scores = score_ref[head] + hidden
        dweights = dweight_ref[head]
        row_max = jnp.max(scores, axis=0, keepdims=True)
        expsum = jnp.exp2((scores - row_max) * exp_scale)
        weights = expsum * (1.0 / jnp.sum(expsum, axis=0, keepdims=True))
        weights_half = weights.astype(jnp.bfloat16)
        delta = jnp.sum(weights_half.astype(jnp.float32) * dweights, axis=0, keepdims=True)
        half_ref[head] = weights_half
        dscore_ref[head] = (weights * (dweights - delta)).astype(jnp.bfloat16)
    for head in range(heads):
        dscore = dscore_ref[head]
        query_grad = lax.dot_general(
            dscore, near(keys, 0, head), tn, preferred_element_type=jnp.float32
        )
        query_grad = (query_grad * score_scale).astype(jnp.bfloat16)
        query_out[head] = query_grad[:tokens]
        if paired:
            other_out[head] = query_grad[tokens:]
        key_part = jnp.dot(dscore, both(query, 0, head), preferred_element_type=jnp.float32)
        value_part = jnp.dot(
            half_ref[head], both(grad, 1, head), preferred_element_type=jnp.float32
        )
        parts = ((key_part * score_scale).astype(jnp.bfloat16), value_part.astype(jnp.bfloat16))
        for side, part in enumerate(parts):
            own_out[side, head] = part[:group_keys]
            for slot, far_out in enumerate(far_outs):
                start = group_keys + slot * KB
                far_out[side, head] = part[start : start + KB]


def step_of(heads, *offsets):
    return max(step for step in range(1, STEP_HEADS + 1) if math.gcd(step, heads, *offsets) == step)


def attend(half, query, grad, keys, values, far, swapped, groups, cut, query_out):
    first_head, heads, paired, _ = cut
    _, tokens, head_dim = query.shape
    group_keys = keys.shape[1]
    masks = far_masks(groups)
    near_keys = group_keys + KB * len(masks)
    if paired:
        heads //= 2
    step_heads = step_of(heads, first_head)
    first_step = first_head // step_heads
    half_steps = heads // step_heads if paired else 0

    def rows(count):
        return pl.BlockSpec(
            (step_heads, count, head_dim),
            lambda i, half: (first_step + half[0] * half_steps + i, 0, 0),
        )

    def pair(count):
        return pl.BlockSpec((2, step_heads, count, head_dim), lambda i, half: (0, i, 0, 0))

    both = pl.BlockSpec((2, 2, step_heads, KB, head_dim), lambda i, half: (0, 0, i, 0, 0))
    block = (2, heads, KB, head_dim)
    shapes = [query.shape, (2, heads, group_keys, head_dim), block]
    shapes += [(2,) + block] * (groups // 2 - 1)
    out_specs = [rows(tokens), pair(group_keys), pair(KB)] + [both] * (groups // 2 - 1)
    operands = [half, query, grad, keys, values, *far]
    in_specs = [rows(tokens), rows(tokens), rows(group_keys), rows(group_keys)]
    in_specs += slot_specs(groups, step_heads, (KB,), head_dim)
    aliases = {}
    if paired:
        operands.append(swapped)
        in_specs.append(pair(tokens))
        shapes.insert(0, (heads, tokens, head_dim))
        out_specs.insert(
            0, pl.BlockSpec((step_heads, tokens, head_dim), lambda i, half: (i, 0, 0))
        )
    if query_out is not None:
        aliases = {len(operands): int(paired)}
        operands.append(query_out)
        in_specs.append(pl.BlockSpec(memory_space=pl.ANY))
    scores = (step_heads, near_keys, tokens * (1 + paired))
    outs = pl.pallas_call(
        functools.partial(attend_kernel, masks, query_out is not None, paired),
        out_shape=[jax.ShapeDtypeStruct(shape, jnp.bfloat16) for shape in shapes],
        grid_spec=pltpu.PrefetchScalarGridSpec(
            num_scalar_prefetch=1,
            grid=(heads // step_heads,),
            in_specs=in_specs,
            out_specs=out_specs,
            scratch_shapes=[pltpu.VMEM(scores, jnp.float32)] * 2
            + [pltpu.VMEM(scores, jnp.bfloat16)] * 2,
        ),
        input_output_aliases=aliases,
        compiler_params=pltpu.CompilerParams(vmem_limit_bytes=VMEM_ATTEND),
        name="attend",
    )(*operands)
    other = None
    if paired:
        other, outs = outs[0], outs[1:]
    return other, outs[0], outs[1], outs[2:]


def merge_kernel(masks, bit, routes, own, *rest):
    slots = len(masks)
    back = rest[:slots]
    sent, kept, total = rest[slots:]
    group = lax.axis_index("blk")
    mine = (lax.axis_index("ulysses") // bit) % 2
    per_block = back[0].shape[2]
    total[...] = own[...].astype(jnp.float32)
    for mask, part in zip(masks, back):
        first = routes[group ^ mask, group] * per_block
        spot = pl.ds(first, per_block)
        total[:, :, spot] = total[:, :, spot] + part[...].astype(jnp.float32)
    for index in range(sent.shape[2]):
        base = index // bit * 2 * bit + index % bit
        for out, side in ((sent, 1 - mine), (kept, mine)):
            out[:, :, index] = total[:, :, base + side * bit].astype(jnp.bfloat16)


def merge(routes, own, back, groups, ranks, bit):
    _, chunk_heads, group_keys, head_dim = own.shape
    rank_keys = group_keys // ranks
    step_heads = step_of(chunk_heads)
    masks = far_masks(groups)
    rows = (KB // rank_keys, rank_keys)

    def blocks(count):
        return pl.BlockSpec(
            (2, step_heads, count, rank_keys, head_dim), lambda i: (0, i, 0, 0, 0)
        )

    half = jax.ShapeDtypeStruct((2, chunk_heads, ranks // 2, rank_keys, head_dim), jnp.bfloat16)
    return pl.pallas_call(
        functools.partial(merge_kernel, masks, bit),
        out_shape=[half, half],
        grid=(chunk_heads // step_heads,),
        in_specs=[pl.BlockSpec(memory_space=pltpu.SMEM), blocks(ranks)]
        + slot_specs(groups, step_heads, rows, head_dim),
        out_specs=[blocks(ranks // 2)] * 2,
        scratch_shapes=[
            pltpu.VMEM((2, step_heads, ranks, rank_keys, head_dim), jnp.float32)
        ],
        compiler_params=pltpu.CompilerParams(vmem_limit_bytes=VMEM_ATTEND),
        name="merge",
    )(
        routes,
        own.reshape(2, chunk_heads, ranks, rank_keys, head_dim),
        *(part.reshape(part.shape[:-2] + rows + (head_dim,)) for part in back),
    )


def body(query_rows, out_grad, key_rows, value_rows, routes):
    head_count, _, head_dim = query_rows.shape
    query_rows, out_grad, key_rows, value_rows, routes = (
        pltpu.with_memory_space_constraint(rows, pltpu.HBM)
        for rows in (query_rows, out_grad, key_rows, value_rows, routes)
    )
    group_keys = key_rows.shape[1]
    groups = lax.axis_size("blk")
    ranks = lax.axis_size("ulysses")
    my_rank = lax.axis_index("ulysses")
    rank_keys = group_keys // ranks
    half = my_rank % 2
    bits = [1 << b for b in range(ranks.bit_length() - 1)]
    whole = sum(parts for _, parts, _, _ in PLAN)
    cuts = [
        (head_count * first // whole, head_count * parts // whole, paired, order)
        for first, parts, paired, order in PLAN
    ]

    def exchange(near, pairs, forward):
        def hop(rows, mask, both=False):
            links = [
                (g, g ^ mask) for g in range(groups) if both or ((g ^ mask) > g) == forward
            ]
            return lax.ppermute(rows, "blk", links)

        crossed = [hop(pair, 2 * i) for i, pair in enumerate(pairs, 1)]
        slots = [hop(near, 1, both=True)]
        for pair in crossed:
            slots += [pair, hop(pair[1], 1, both=True)]
        return slots

    def scatter(sent, kept, order):
        left = list(reversed(bits))
        for step, bit in enumerate(order):
            left.remove(bit)
            if step:
                axis = 2 + sum(b > bit for b in left)
                mine = (my_rank // bit) % 2
                sent = lax.dynamic_index_in_dim(total, 1 - mine, axis, keepdims=False)
                kept = lax.dynamic_index_in_dim(total, mine, axis, keepdims=False)
            came = lax.ppermute(sent, "ulysses", [(r, r ^ bit) for r in range(ranks)])
            total = kept.astype(jnp.float32) + came.astype(jnp.float32)
            total = total.reshape(kept.shape[:2] + (2,) * len(left) + (rank_keys, head_dim))
            if step + 1 < len(order):
                total = total.astype(jnp.bfloat16)
        return total

    def trade(rows):
        return lax.ppermute(rows, "ulysses", [(r, r ^ 1) for r in range(ranks)])

    def join(total):
        mine = lax.dynamic_index_in_dim(total, half, 2, keepdims=False)
        away = lax.dynamic_index_in_dim(total, 1 - half, 2, keepdims=False)
        came = trade(away.astype(jnp.bfloat16)).astype(jnp.float32)
        low = jnp.where(half == 0, mine, came)
        high = jnp.where(half == 0, came, mine)
        return jnp.concatenate([low, high], axis=1)

    half_operand = half.astype(jnp.int32).reshape(1)
    picked = pick(routes, query_rows, out_grad, key_rows, value_rows, groups, cuts)
    query_out = None
    results = []
    others = []
    fetched = []
    for swapped, parts in picked:
        if swapped is not None:
            swapped = trade(swapped)
        fetched.append((swapped, exchange(parts[0], parts[1:], True)))
    for number, cut in enumerate(cuts):
        swapped, far = fetched[number]
        other, query_out, own, parts = attend(
            half_operand, query_rows, out_grad, key_rows, value_rows, far, swapped,
            groups, cut, query_out,
        )
        back = exchange(parts[0], parts[1:], False)
        if other is not None:
            others.append((cut, trade(other)))
        order = [bit for bit in bits if not (cut[2] and bit == 1)]
        if cut[3]:
            order[0], order[1] = order[1], order[0]
        sent, kept = merge(routes, own, back, groups, ranks, order[0])
        total = scatter(sent, kept, order)
        results.append(join(total) if cut[2] else total)
    for cut, rows in others:
        first = cut[0] + (1 - half) * (cut[1] // 2)
        query_out = lax.dynamic_update_slice_in_dim(query_out, rows, first, 0)
    placed = [results[number] for number in sorted(range(len(cuts)), key=lambda n: cuts[n][0])]
    key_grad = jnp.concatenate([total[0] for total in placed], axis=0)
    value_grad = jnp.concatenate([total[1] for total in placed], axis=0)
    return (query_out, key_grad, value_grad)


def solution(mesh):
    return jax.shard_map(
        body,
        mesh=mesh,
        in_specs=(
            P(None, ("blk", "ulysses"), None),
            P(None, ("blk", "ulysses"), None),
            P(None, "blk", None),
            P(None, "blk", None),
            P(),
        ),
        out_specs=(
            P(None, ("blk", "ulysses"), None),
            P(None, ("blk", "ulysses"), None),
            P(None, ("blk", "ulysses"), None),
        ),
        check_vma=False,
    )
```

```python
import functools
import math

import jax
import jax.numpy as jnp
from jax import lax
from jax.experimental import pallas as pl
from jax.experimental.pallas import tpu as pltpu
from jax.sharding import PartitionSpec as P


KB = 16
PLAN = ((16, 16, False, (1, 2)), (0, 16, True, (2,)))
STEP_HEADS = 8
VMEM_SMALL = 8 << 20
VMEM_ATTEND = 24 << 20


def far_masks(groups):
    return [1] + [mask for even in range(2, groups, 2) for mask in (even, even ^ 1)]


def pick_kernel(cuts, groups, routes, query, grad, keys, values, *rest):
    outs, arrived = list(rest[:-1]), rest[-1]
    group = lax.axis_index("blk")
    half = lax.axis_index("ulysses") % 2
    copies = []
    for number, (first_head, heads, paired, _) in enumerate(cuts):
        if paired:
            heads //= 2
            other = first_head + (1 - half) * heads
            first_head = first_head + half * heads
            swapped = outs.pop(0)
            for side, rows in enumerate((query, grad)):
                copies.append(
                    pltpu.make_async_copy(
                        rows.at[pl.ds(other, heads)],
                        swapped.at[side],
                        arrived.at[number, groups - 1, side],
                    )
                )
        for index, mask in enumerate(far_masks(groups)):
            out = outs[(index + 1) // 2]
            out = out if index == 0 else out.at[(index + 1) % 2]
            start = pl.multiple_of(routes[group ^ mask, group] * KB, KB)
            for side, rows in enumerate((keys, values)):
                copies.append(
                    pltpu.make_async_copy(
                        rows.at[pl.ds(first_head, heads), pl.ds(start, KB)],
                        out.at[side],
                        arrived.at[number, index, side],
                    )
                )
        outs = outs[groups // 2 :]
    for copy in copies:
        copy.start()
    for copy in copies:
        copy.wait()


def pick(routes, query, grad, keys, values, groups, cuts):
    _, tokens, head_dim = query.shape
    shapes, counts = [], []
    for _, heads, paired, _ in cuts:
        heads = heads // 2 if paired else heads
        block = (2, heads, KB, head_dim)
        swap = [(2, heads, tokens, head_dim)] if paired else []
        shapes += swap + [block] + [(2,) + block] * (groups // 2 - 1)
        counts.append(len(swap) + groups // 2)
    outs = pl.pallas_call(
        functools.partial(pick_kernel, cuts, groups),
        out_shape=[jax.ShapeDtypeStruct(shape, jnp.bfloat16) for shape in shapes],
        in_specs=[pl.BlockSpec(memory_space=pltpu.SMEM)]
        + [pl.BlockSpec(memory_space=pltpu.HBM)] * 4,
        out_specs=[pl.BlockSpec(memory_space=pltpu.VMEM)] * len(shapes),
        scratch_shapes=[pltpu.SemaphoreType.DMA((len(cuts), groups, 2))],
        compiler_params=pltpu.CompilerParams(vmem_limit_bytes=VMEM_SMALL),
        name="pick",
    )(routes, query, grad, keys, values)
    picked = []
    for count, cut in zip(counts, cuts):
        mine, outs = outs[:count], outs[count:]
        picked.append((mine[0], mine[1:]) if cut[2] else (None, mine))
    return picked


def slot_specs(groups, step_heads, rows, head_dim):
    flat = pl.BlockSpec((2, step_heads) + rows + (head_dim,), lambda i, *_: (0, i) + (0,) * (len(rows) + 1))
    half = pl.BlockSpec(
        (None, 2, step_heads) + rows + (head_dim,), lambda i, *_: (0, 0, i) + (0,) * (len(rows) + 1)
    )
    return [flat] + [half, flat] * (groups // 2 - 1)


def attend_kernel(masks, has_alias, paired, _, query, grad, keys, values, *rest):
    slots = len(masks)
    far_rows = rest[:slots]
    swapped = rest[slots] if paired else None
    rest = rest[slots + has_alias + paired :]
    if paired:
        other_out, rest = rest[0], rest[1:]
    query_out, own_out, near_out = rest[:3]
    pair_outs = rest[3 : 3 + slots // 2]
    far_outs = [near_out] + [out.at[half] for out in pair_outs for half in range(2)]
    score_ref, dweight_ref, half_ref, dscore_ref = rest[3 + slots // 2 :]
    heads, tokens, head_dim = query.shape
    group_keys = keys.shape[1]
    group = lax.axis_index("blk")
    rank = lax.axis_index("ulysses")
    key_stride = tokens * lax.axis_size("ulysses") // group_keys
    score_scale = 1.0 / math.sqrt(head_dim)
    exp_scale = score_scale * math.log2(math.e)
    key_at = lax.broadcasted_iota(jnp.int32, (group_keys, tokens), 0) * key_stride
    token_at = lax.broadcasted_iota(jnp.int32, (group_keys, tokens), 1)
    sources = (rank, rank ^ 1) if paired else (rank,)
    hidden = [
        jnp.concatenate(
            [jnp.where(key_at <= token_at + source * tokens, 0.0, -jnp.inf) for source in sources],
            axis=1,
        )
    ]
    for mask in masks:
        seen = jnp.where((group ^ mask) < group, 0.0, -jnp.inf)
        hidden.append(jnp.full((KB, tokens * len(sources)), seen, jnp.float32))
    hidden = jnp.concatenate(hidden, axis=0)
    nt = (((1,), (1,)), ((), ()))
    tn = (((0,), (0,)), ((), ()))

    def near(rows, side, head):
        return jnp.concatenate([rows[head]] + [far[side, head] for far in far_rows], axis=0)

    def both(rows, side, head):
        if not paired:
            return rows[head]
        return jnp.concatenate([rows[head], swapped[side, head]], axis=0)

    for head in range(heads):
        score_ref[head] = lax.dot_general(
            near(keys, 0, head), both(query, 0, head), nt, preferred_element_type=jnp.float32
        )
        dweight_ref[head] = lax.dot_general(
            near(values, 1, head), both(grad, 1, head), nt, preferred_element_type=jnp.float32
        )
    for head in range(heads):
        scores = score_ref[head] + hidden
        dweights = dweight_ref[head]
        row_max = jnp.max(scores, axis=0, keepdims=True)
        expsum = jnp.exp2((scores - row_max) * exp_scale)
        weights = expsum * (1.0 / jnp.sum(expsum, axis=0, keepdims=True))
        weights_half = weights.astype(jnp.bfloat16)
        delta = jnp.sum(weights_half.astype(jnp.float32) * dweights, axis=0, keepdims=True)
        half_ref[head] = weights_half
        dscore_ref[head] = (weights * (dweights - delta)).astype(jnp.bfloat16)
    for head in range(heads):
        dscore = dscore_ref[head]
        query_grad = lax.dot_general(
            dscore, near(keys, 0, head), tn, preferred_element_type=jnp.float32
        )
        query_grad = (query_grad * score_scale).astype(jnp.bfloat16)
        query_out[head] = query_grad[:tokens]
        if paired:
            other_out[head] = query_grad[tokens:]
        key_part = jnp.dot(dscore, both(query, 0, head), preferred_element_type=jnp.float32)
        value_part = jnp.dot(
            half_ref[head], both(grad, 1, head), preferred_element_type=jnp.float32
        )
        parts = ((key_part * score_scale).astype(jnp.bfloat16), value_part.astype(jnp.bfloat16))
        for side, part in enumerate(parts):
            own_out[side, head] = part[:group_keys]
            for slot, far_out in enumerate(far_outs):
                start = group_keys + slot * KB
                far_out[side, head] = part[start : start + KB]


def step_of(heads, *offsets):
    return max(step for step in range(1, STEP_HEADS + 1) if math.gcd(step, heads, *offsets) == step)


def attend(half, query, grad, keys, values, far, swapped, groups, cut, query_out):
    first_head, heads, paired, _ = cut
    _, tokens, head_dim = query.shape
    group_keys = keys.shape[1]
    masks = far_masks(groups)
    near_keys = group_keys + KB * len(masks)
    if paired:
        heads //= 2
    step_heads = step_of(heads, first_head)
    first_step = first_head // step_heads
    half_steps = heads // step_heads if paired else 0

    def rows(count):
        return pl.BlockSpec(
            (step_heads, count, head_dim),
            lambda i, half: (first_step + half[0] * half_steps + i, 0, 0),
        )

    def pair(count):
        return pl.BlockSpec((2, step_heads, count, head_dim), lambda i, half: (0, i, 0, 0))

    both = pl.BlockSpec((2, 2, step_heads, KB, head_dim), lambda i, half: (0, 0, i, 0, 0))
    block = (2, heads, KB, head_dim)
    shapes = [query.shape, (2, heads, group_keys, head_dim), block]
    shapes += [(2,) + block] * (groups // 2 - 1)
    out_specs = [rows(tokens), pair(group_keys), pair(KB)] + [both] * (groups // 2 - 1)
    operands = [half, query, grad, keys, values, *far]
    in_specs = [rows(tokens), rows(tokens), rows(group_keys), rows(group_keys)]
    in_specs += slot_specs(groups, step_heads, (KB,), head_dim)
    aliases = {}
    if paired:
        operands.append(swapped)
        in_specs.append(pair(tokens))
        shapes.insert(0, (heads, tokens, head_dim))
        out_specs.insert(
            0, pl.BlockSpec((step_heads, tokens, head_dim), lambda i, half: (i, 0, 0))
        )
    if query_out is not None:
        aliases = {len(operands): int(paired)}
        operands.append(query_out)
        in_specs.append(pl.BlockSpec(memory_space=pl.ANY))
    scores = (step_heads, near_keys, tokens * (1 + paired))
    outs = pl.pallas_call(
        functools.partial(attend_kernel, masks, query_out is not None, paired),
        out_shape=[jax.ShapeDtypeStruct(shape, jnp.bfloat16) for shape in shapes],
        grid_spec=pltpu.PrefetchScalarGridSpec(
            num_scalar_prefetch=1,
            grid=(heads // step_heads,),
            in_specs=in_specs,
            out_specs=out_specs,
            scratch_shapes=[pltpu.VMEM(scores, jnp.float32)] * 2
            + [pltpu.VMEM(scores, jnp.bfloat16)] * 2,
        ),
        input_output_aliases=aliases,
        compiler_params=pltpu.CompilerParams(vmem_limit_bytes=VMEM_ATTEND),
        name="attend",
    )(*operands)
    other = None
    if paired:
        other, outs = outs[0], outs[1:]
    return other, outs[0], outs[1], outs[2:]


def mixes(bits):
    found = [0]
    for bit in bits:
        found += [mask | bit for mask in found]
    return found


def merge_kernel(masks, bits, routes, own, *rest):
    slots = len(masks)
    back = rest[:slots]
    outs, total = rest[slots:-1], rest[-1]
    group = lax.axis_index("blk")
    rank = lax.axis_index("ulysses")
    per_block = back[0].shape[2]
    total[...] = own[...].astype(jnp.float32)
    for mask, part in zip(masks, back):
        first = routes[group ^ mask, group] * per_block
        spot = pl.ds(first, per_block)
        total[:, :, spot] = total[:, :, spot] + part[...].astype(jnp.float32)
    chosen = sum(bits)
    bases = [index for index in range(own.shape[2]) if index & chosen == 0]
    for mix, out in zip(mixes(bits), outs):
        for index, base in enumerate(bases):
            out[:, :, index] = total[:, :, base + ((rank ^ mix) & chosen)].astype(jnp.bfloat16)


def merge(routes, own, back, groups, ranks, bits):
    _, chunk_heads, group_keys, head_dim = own.shape
    rank_keys = group_keys // ranks
    step_heads = step_of(chunk_heads)
    masks = far_masks(groups)
    rows = (KB // rank_keys, rank_keys)

    def blocks(count):
        return pl.BlockSpec(
            (2, step_heads, count, rank_keys, head_dim), lambda i: (0, i, 0, 0, 0)
        )

    pieces = 1 << len(bits)
    piece = (2, chunk_heads, ranks // pieces, rank_keys, head_dim)
    return pl.pallas_call(
        functools.partial(merge_kernel, masks, bits),
        out_shape=[jax.ShapeDtypeStruct(piece, jnp.bfloat16)] * pieces,
        grid=(chunk_heads // step_heads,),
        in_specs=[pl.BlockSpec(memory_space=pltpu.SMEM), blocks(ranks)]
        + slot_specs(groups, step_heads, rows, head_dim),
        out_specs=[blocks(ranks // pieces)] * pieces,
        scratch_shapes=[
            pltpu.VMEM((2, step_heads, ranks, rank_keys, head_dim), jnp.float32)
        ],
        compiler_params=pltpu.CompilerParams(vmem_limit_bytes=VMEM_ATTEND),
        name="merge",
    )(
        routes,
        own.reshape(2, chunk_heads, ranks, rank_keys, head_dim),
        *(part.reshape(part.shape[:-2] + rows + (head_dim,)) for part in back),
    )


def body(query_rows, out_grad, key_rows, value_rows, routes):
    head_count, _, head_dim = query_rows.shape
    query_rows, out_grad, key_rows, value_rows, routes = (
        pltpu.with_memory_space_constraint(rows, pltpu.HBM)
        for rows in (query_rows, out_grad, key_rows, value_rows, routes)
    )
    group_keys = key_rows.shape[1]
    groups = lax.axis_size("blk")
    ranks = lax.axis_size("ulysses")
    my_rank = lax.axis_index("ulysses")
    rank_keys = group_keys // ranks
    half = my_rank % 2
    bits = [1 << b for b in range(ranks.bit_length() - 1)]
    whole = sum(parts for _, parts, _, _ in PLAN)
    cuts = [
        (head_count * first // whole, head_count * parts // whole, paired, order)
        for first, parts, paired, order in PLAN
    ]

    def exchange(near, pairs, forward):
        def hop(rows, mask, both=False):
            links = [
                (g, g ^ mask) for g in range(groups) if both or ((g ^ mask) > g) == forward
            ]
            return lax.ppermute(rows, "blk", links)

        crossed = [hop(pair, 2 * i) for i, pair in enumerate(pairs, 1)]
        slots = [hop(near, 1, both=True)]
        for pair in crossed:
            slots += [pair, hop(pair[1], 1, both=True)]
        return slots

    def scatter(pieces, stages):
        left = [bit for bit in bits]
        for step, stage in enumerate(stages):
            left = [bit for bit in left if bit not in stage]
            shape = (2, pieces[0].shape[1]) + (2,) * len(left) + (rank_keys, head_dim)
            came = [
                lax.ppermute(piece.reshape(shape), "ulysses", [(r, r ^ mix) for r in range(ranks)])
                for mix, piece in zip(mixes(stage)[1:], pieces[1:])
            ]
            total = pieces[0].reshape(shape).astype(jnp.float32)
            for part in came:
                total = total + part.astype(jnp.float32)
            if step + 1 == len(stages):
                return total
            total = total.astype(jnp.bfloat16)
            after = stages[step + 1]
            rest = [bit for bit in left if bit not in after]
            axes = [2 + sum(b > bit for b in rest + list(after)) for bit in after]
            pieces = []
            for mix in mixes(after):
                starts = [0] * total.ndim
                sizes = list(total.shape)
                for bit, axis in zip(after, axes):
                    starts[axis] = ((my_rank ^ mix) // bit) % 2
                    sizes[axis] = 1
                pieces.append(lax.dynamic_slice(total, starts, sizes))

    def trade(rows):
        return lax.ppermute(rows, "ulysses", [(r, r ^ 1) for r in range(ranks)])

    def join(total):
        mine = lax.dynamic_index_in_dim(total, half, 2, keepdims=False)
        away = lax.dynamic_index_in_dim(total, 1 - half, 2, keepdims=False)
        came = trade(away.astype(jnp.bfloat16)).astype(jnp.float32)
        low = jnp.where(half == 0, mine, came)
        high = jnp.where(half == 0, came, mine)
        return jnp.concatenate([low, high], axis=1)

    half_operand = half.astype(jnp.int32).reshape(1)
    picked = pick(routes, query_rows, out_grad, key_rows, value_rows, groups, cuts)
    query_out = None
    results = []
    others = []
    fetched = []
    for swapped, parts in picked:
        if swapped is not None:
            swapped = trade(swapped)
        fetched.append((swapped, exchange(parts[0], parts[1:], True)))
    for number, cut in enumerate(cuts):
        swapped, far = fetched[number]
        other, query_out, own, parts = attend(
            half_operand, query_rows, out_grad, key_rows, value_rows, far, swapped,
            groups, cut, query_out,
        )
        back = exchange(parts[0], parts[1:], False)
        if other is not None:
            others.append((cut, trade(other)))
        wanted = [bit for bit in bits if not (cut[2] and bit == 1)]
        stages = []
        for size in cut[3] + (1,) * len(bits):
            if wanted:
                stages.append(tuple(wanted[:size]))
                wanted = wanted[size:]
        pieces = merge(routes, own, back, groups, ranks, stages[0])
        total = scatter(pieces, stages)
        results.append(join(total) if cut[2] else total)
    for cut, rows in others:
        first = cut[0] + (1 - half) * (cut[1] // 2)
        query_out = lax.dynamic_update_slice_in_dim(query_out, rows, first, 0)
    placed = [results[number] for number in sorted(range(len(cuts)), key=lambda n: cuts[n][0])]
    key_grad = jnp.concatenate([total[0] for total in placed], axis=0)
    value_grad = jnp.concatenate([total[1] for total in placed], axis=0)
    return (query_out, key_grad, value_grad)


def solution(mesh):
    return jax.shard_map(
        body,
        mesh=mesh,
        in_specs=(
            P(None, ("blk", "ulysses"), None),
            P(None, ("blk", "ulysses"), None),
            P(None, "blk", None),
            P(None, "blk", None),
            P(),
        ),
        out_specs=(
            P(None, ("blk", "ulysses"), None),
            P(None, ("blk", "ulysses"), None),
            P(None, ("blk", "ulysses"), None),
        ),
        check_vma=False,
    )
```

```python
import functools
import math

import jax
import jax.numpy as jnp
from jax import lax
from jax.experimental import pallas as pl
from jax.experimental.pallas import tpu as pltpu
from jax.sharding import PartitionSpec as P


KB = 16
PLAN = ((16, 16, False, (1, 2)), (0, 16, True, (2,)))
STEP_HEADS = 8
VMEM_SMALL = 8 << 20
VMEM_ATTEND = 16 << 20


def far_masks(groups):
    return [1] + [mask for even in range(2, groups, 2) for mask in (even, even ^ 1)]


def pick_kernel(cuts, groups, routes, query, grad, keys, values, *rest):
    outs, arrived = list(rest[:-1]), rest[-1]
    group = lax.axis_index("blk")
    half = lax.axis_index("ulysses") % 2
    copies = []
    for number, (first_head, heads, paired, _) in enumerate(cuts):
        if paired:
            heads //= 2
            other = first_head + (1 - half) * heads
            first_head = first_head + half * heads
            swapped = outs.pop(0)
            for side, rows in enumerate((query, grad)):
                copies.append(
                    pltpu.make_async_copy(
                        rows.at[pl.ds(other, heads)],
                        swapped.at[side],
                        arrived.at[number, groups - 1, side],
                    )
                )
        for index, mask in enumerate(far_masks(groups)):
            out = outs[(index + 1) // 2]
            out = out if index == 0 else out.at[(index + 1) % 2]
            start = pl.multiple_of(routes[group ^ mask, group] * KB, KB)
            for side, rows in enumerate((keys, values)):
                copies.append(
                    pltpu.make_async_copy(
                        rows.at[pl.ds(first_head, heads), pl.ds(start, KB)],
                        out.at[side],
                        arrived.at[number, index, side],
                    )
                )
        outs = outs[groups // 2 :]
    for copy in copies:
        copy.start()
    for copy in copies:
        copy.wait()


def pick(routes, query, grad, keys, values, groups, cuts):
    _, tokens, head_dim = query.shape
    shapes, counts = [], []
    for _, heads, paired, _ in cuts:
        heads = heads // 2 if paired else heads
        block = (2, heads, KB, head_dim)
        swap = [(2, heads, tokens, head_dim)] if paired else []
        shapes += swap + [block] + [(2,) + block] * (groups // 2 - 1)
        counts.append(len(swap) + groups // 2)
    outs = pl.pallas_call(
        functools.partial(pick_kernel, cuts, groups),
        out_shape=[jax.ShapeDtypeStruct(shape, jnp.bfloat16) for shape in shapes],
        in_specs=[pl.BlockSpec(memory_space=pltpu.SMEM)]
        + [pl.BlockSpec(memory_space=pltpu.HBM)] * 4,
        out_specs=[pl.BlockSpec(memory_space=pltpu.VMEM)] * len(shapes),
        scratch_shapes=[pltpu.SemaphoreType.DMA((len(cuts), groups, 2))],
        compiler_params=pltpu.CompilerParams(vmem_limit_bytes=VMEM_SMALL),
        name="pick",
    )(routes, query, grad, keys, values)
    picked = []
    for count, cut in zip(counts, cuts):
        mine, outs = outs[:count], outs[count:]
        picked.append((mine[0], mine[1:]) if cut[2] else (None, mine))
    return picked


def slot_specs(groups, step_heads, rows, head_dim):
    flat = pl.BlockSpec((2, step_heads) + rows + (head_dim,), lambda i, *_: (0, i) + (0,) * (len(rows) + 1))
    half = pl.BlockSpec(
        (None, 2, step_heads) + rows + (head_dim,), lambda i, *_: (0, 0, i) + (0,) * (len(rows) + 1)
    )
    return [flat] + [half, flat] * (groups // 2 - 1)


def attend_kernel(masks, has_alias, paired, _, query, grad, keys, values, *rest):
    slots = len(masks)
    far_rows = rest[:slots]
    swapped = rest[slots] if paired else None
    rest = rest[slots + has_alias + paired :]
    if paired:
        other_out, rest = rest[0], rest[1:]
    query_out, own_out, near_out = rest[:3]
    pair_outs = rest[3 : 3 + slots // 2]
    far_outs = [near_out] + [out.at[half] for out in pair_outs for half in range(2)]
    score_ref, dweight_ref, half_ref, dscore_ref = rest[3 + slots // 2 :]
    heads, tokens, head_dim = query.shape
    group_keys = keys.shape[1]
    group = lax.axis_index("blk")
    rank = lax.axis_index("ulysses")
    key_stride = tokens * lax.axis_size("ulysses") // group_keys
    score_scale = 1.0 / math.sqrt(head_dim)
    exp_scale = score_scale * math.log2(math.e)
    key_at = lax.broadcasted_iota(jnp.int32, (group_keys, tokens), 0) * key_stride
    token_at = lax.broadcasted_iota(jnp.int32, (group_keys, tokens), 1)
    sources = (rank, rank ^ 1) if paired else (rank,)
    hidden = [
        jnp.concatenate(
            [jnp.where(key_at <= token_at + source * tokens, 0.0, -jnp.inf) for source in sources],
            axis=1,
        )
    ]
    for mask in masks:
        seen = jnp.where((group ^ mask) < group, 0.0, -jnp.inf)
        hidden.append(jnp.full((KB, tokens * len(sources)), seen, jnp.float32))
    hidden = jnp.concatenate(hidden, axis=0)
    nt = (((1,), (1,)), ((), ()))
    tn = (((0,), (0,)), ((), ()))

    def near(rows, side, head):
        return jnp.concatenate([rows[head]] + [far[side, head] for far in far_rows], axis=0)

    def both(rows, side, head):
        if not paired:
            return rows[head]
        return jnp.concatenate([rows[head], swapped[side, head]], axis=0)

    for head in range(heads):
        score_ref[head] = lax.dot_general(
            near(keys, 0, head), both(query, 0, head), nt, preferred_element_type=jnp.float32
        )
        dweight_ref[head] = lax.dot_general(
            near(values, 1, head), both(grad, 1, head), nt, preferred_element_type=jnp.float32
        )
    for head in range(heads):
        scores = score_ref[head] + hidden
        dweights = dweight_ref[head]
        row_max = jnp.max(scores, axis=0, keepdims=True)
        expsum = jnp.exp2((scores - row_max) * exp_scale)
        weights = expsum * (1.0 / jnp.sum(expsum, axis=0, keepdims=True))
        weights_half = weights.astype(jnp.bfloat16)
        delta = jnp.sum(weights_half.astype(jnp.float32) * dweights, axis=0, keepdims=True)
        half_ref[head] = weights_half
        dscore_ref[head] = (weights * (dweights - delta)).astype(jnp.bfloat16)
    for head in range(heads):
        dscore = dscore_ref[head]
        query_grad = lax.dot_general(
            dscore, near(keys, 0, head), tn, preferred_element_type=jnp.float32
        )
        query_grad = (query_grad * score_scale).astype(jnp.bfloat16)
        query_out[head] = query_grad[:tokens]
        if paired:
            other_out[head] = query_grad[tokens:]
        key_part = jnp.dot(dscore, both(query, 0, head), preferred_element_type=jnp.float32)
        value_part = jnp.dot(
            half_ref[head], both(grad, 1, head), preferred_element_type=jnp.float32
        )
        parts = ((key_part * score_scale).astype(jnp.bfloat16), value_part.astype(jnp.bfloat16))
        for side, part in enumerate(parts):
            own_out[side, head] = part[:group_keys]
            for slot, far_out in enumerate(far_outs):
                start = group_keys + slot * KB
                far_out[side, head] = part[start : start + KB]


def step_of(heads, *offsets):
    return max(step for step in range(1, STEP_HEADS + 1) if math.gcd(step, heads, *offsets) == step)


def attend(half, rows, far, swapped, groups, cut, query_shape, query_out):
    first_head, heads, paired, _ = cut
    _, tokens, head_dim = query_shape
    group_keys = rows[2].shape[1]
    masks = far_masks(groups)
    near_keys = group_keys + KB * len(masks)
    if paired:
        heads //= 2
    step_heads = step_of(heads, first_head)
    first_step = first_head // step_heads
    half_steps = heads // step_heads if paired else 0

    def placed(count):
        return pl.BlockSpec(
            (step_heads, count, head_dim),
            lambda i, half: (first_step + half[0] * half_steps + i, 0, 0),
        )

    def pair(count):
        return pl.BlockSpec((2, step_heads, count, head_dim), lambda i, half: (0, i, 0, 0))

    both = pl.BlockSpec((2, 2, step_heads, KB, head_dim), lambda i, half: (0, 0, i, 0, 0))
    block = (2, heads, KB, head_dim)
    shapes = [query_shape, (2, heads, group_keys, head_dim), block]
    shapes += [(2,) + block] * (groups // 2 - 1)
    out_specs = [placed(tokens), pair(group_keys), pair(KB)] + [both] * (groups // 2 - 1)
    operands = [half, *rows, *far]
    in_specs = [placed(tokens)] * 2 + [placed(group_keys)] * 2
    in_specs += slot_specs(groups, step_heads, (KB,), head_dim)
    aliases = {}
    if paired:
        operands.append(swapped)
        in_specs.append(pair(tokens))
        shapes.insert(0, (heads, tokens, head_dim))
        out_specs.insert(
            0, pl.BlockSpec((step_heads, tokens, head_dim), lambda i, half: (i, 0, 0))
        )
    if query_out is not None:
        aliases = {len(operands): int(paired)}
        operands.append(query_out)
        in_specs.append(pl.BlockSpec(memory_space=pl.ANY))
    scores = (step_heads, near_keys, tokens * (1 + paired))
    outs = pl.pallas_call(
        functools.partial(attend_kernel, masks, query_out is not None, paired),
        out_shape=[jax.ShapeDtypeStruct(shape, jnp.bfloat16) for shape in shapes],
        grid_spec=pltpu.PrefetchScalarGridSpec(
            num_scalar_prefetch=1,
            grid=(heads // step_heads,),
            in_specs=in_specs,
            out_specs=out_specs,
            scratch_shapes=[pltpu.VMEM(scores, jnp.float32)] * 2
            + [pltpu.VMEM(scores, jnp.bfloat16)] * 2,
        ),
        input_output_aliases=aliases,
        compiler_params=pltpu.CompilerParams(vmem_limit_bytes=VMEM_ATTEND),
        name="attend",
    )(*operands)
    other = None
    if paired:
        other, outs = outs[0], outs[1:]
    return other, outs[0], outs[1], outs[2:]


def mixes(bits):
    found = [0]
    for bit in bits:
        found += [mask | bit for mask in found]
    return found


def merge_kernel(masks, bits, routes, own, *rest):
    slots = len(masks)
    back = rest[:slots]
    outs, total = rest[slots:-1], rest[-1]
    group = lax.axis_index("blk")
    rank = lax.axis_index("ulysses")
    per_block = back[0].shape[2]
    total[...] = own[...].astype(jnp.float32)
    for mask, part in zip(masks, back):
        first = routes[group ^ mask, group] * per_block
        spot = pl.ds(first, per_block)
        total[:, :, spot] = total[:, :, spot] + part[...].astype(jnp.float32)
    chosen = sum(bits)
    bases = [index for index in range(own.shape[2]) if index & chosen == 0]
    for mix, out in zip(mixes(bits), outs):
        for index, base in enumerate(bases):
            out[:, :, index] = total[:, :, base + ((rank ^ mix) & chosen)].astype(jnp.bfloat16)


def merge(routes, own, back, groups, ranks, bits):
    _, chunk_heads, group_keys, head_dim = own.shape
    rank_keys = group_keys // ranks
    step_heads = step_of(chunk_heads)
    masks = far_masks(groups)
    rows = (KB // rank_keys, rank_keys)

    def blocks(count):
        return pl.BlockSpec(
            (2, step_heads, count, rank_keys, head_dim), lambda i: (0, i, 0, 0, 0)
        )

    pieces = 1 << len(bits)
    piece = (2, chunk_heads, ranks // pieces, rank_keys, head_dim)
    return pl.pallas_call(
        functools.partial(merge_kernel, masks, bits),
        out_shape=[jax.ShapeDtypeStruct(piece, jnp.bfloat16)] * pieces,
        grid=(chunk_heads // step_heads,),
        in_specs=[pl.BlockSpec(memory_space=pltpu.SMEM), blocks(ranks)]
        + slot_specs(groups, step_heads, rows, head_dim),
        out_specs=[blocks(ranks // pieces)] * pieces,
        scratch_shapes=[
            pltpu.VMEM((2, step_heads, ranks, rank_keys, head_dim), jnp.float32)
        ],
        compiler_params=pltpu.CompilerParams(vmem_limit_bytes=VMEM_ATTEND),
        name="merge",
    )(
        routes,
        own.reshape(2, chunk_heads, ranks, rank_keys, head_dim),
        *(part.reshape(part.shape[:-2] + rows + (head_dim,)) for part in back),
    )


def body(query_rows, out_grad, key_rows, value_rows, routes):
    head_count, _, head_dim = query_rows.shape
    query_rows, out_grad, key_rows, value_rows, routes = (
        pltpu.with_memory_space_constraint(rows, pltpu.HBM)
        for rows in (query_rows, out_grad, key_rows, value_rows, routes)
    )
    group_keys = key_rows.shape[1]
    groups = lax.axis_size("blk")
    ranks = lax.axis_size("ulysses")
    my_rank = lax.axis_index("ulysses")
    rank_keys = group_keys // ranks
    half = my_rank % 2
    bits = [1 << b for b in range(ranks.bit_length() - 1)]
    whole = sum(parts for _, parts, _, _ in PLAN)
    cuts = [
        (head_count * first // whole, head_count * parts // whole, paired, order)
        for first, parts, paired, order in PLAN
    ]

    def exchange(near, pairs):
        def hop(rows, mask):
            return lax.ppermute(rows, "blk", [(g, g ^ mask) for g in range(groups)])

        crossed = [hop(pair, 2 * i) for i, pair in enumerate(pairs, 1)]
        slots = [hop(near, 1)]
        for pair in crossed:
            slots += [pair, hop(pair[1], 1)]
        return slots

    def scatter(pieces, stages):
        left = [bit for bit in bits]
        for step, stage in enumerate(stages):
            left = [bit for bit in left if bit not in stage]
            shape = (2, pieces[0].shape[1]) + (2,) * len(left) + (rank_keys, head_dim)
            came = []
            for mix, piece in zip(mixes(stage)[1:], pieces[1:]):
                came.append(
                    lax.ppermute(
                        piece.reshape(shape), "ulysses", [(r, r ^ mix) for r in range(ranks)]
                    )
                )
            total = pieces[0].reshape(shape).astype(jnp.float32)
            for part in came:
                total = total + part.astype(jnp.float32)
            if step + 1 == len(stages):
                return total
            total = total.astype(jnp.bfloat16)
            after = stages[step + 1]
            rest = [bit for bit in left if bit not in after]
            axes = [2 + sum(b > bit for b in rest + list(after)) for bit in after]
            pieces = []
            for mix in mixes(after):
                starts = [0] * total.ndim
                sizes = list(total.shape)
                for bit, axis in zip(after, axes):
                    starts[axis] = ((my_rank ^ mix) // bit) % 2
                    sizes[axis] = 1
                pieces.append(lax.dynamic_slice(total, starts, sizes))

    def trade(rows):
        return lax.ppermute(rows, "ulysses", [(r, r ^ 1) for r in range(ranks)])

    def join(total):
        mine = lax.dynamic_index_in_dim(total, half, 2, keepdims=False)
        away = lax.dynamic_index_in_dim(total, 1 - half, 2, keepdims=False)
        came = trade(away.astype(jnp.bfloat16)).astype(jnp.float32)
        low = jnp.where(half == 0, mine, came)
        high = jnp.where(half == 0, came, mine)
        return jnp.concatenate([low, high], axis=1)

    half_operand = half.astype(jnp.int32).reshape(1)
    picked = pick(routes, query_rows, out_grad, key_rows, value_rows, groups, cuts)
    local_rows = (query_rows, out_grad, key_rows, value_rows)
    query_out = None
    results = []
    others = []
    fetched = []
    for swapped, parts in picked:
        if swapped is not None:
            swapped = trade(swapped)
        fetched.append((swapped, exchange(parts[0], parts[1:])))
    for number, cut in enumerate(cuts):
        swapped, far = fetched[number]
        other, query_out, own, parts = attend(
            half_operand, local_rows, far, swapped, groups, cut, query_rows.shape, query_out
        )
        back = exchange(parts[0], parts[1:])
        if other is not None:
            others.append((cut, trade(other)))
        wanted = [bit for bit in bits if not (cut[2] and bit == 1)]
        stages = []
        for size in cut[3] + (1,) * len(bits):
            if wanted:
                stages.append(tuple(wanted[:size]))
                wanted = wanted[size:]
        pieces = merge(routes, own, back, groups, ranks, stages[0])
        total = scatter(pieces, stages)
        if cut[2]:
            total = join(total)
        results.append(total)
    for cut, rows in others:
        first = cut[0] + (1 - half) * (cut[1] // 2)
        query_out = lax.dynamic_update_slice_in_dim(query_out, rows, first, 0)
    order = sorted(range(len(cuts)), key=lambda number: cuts[number][0])
    grads = []
    for side in range(2):
        base = lax.optimization_barrier(
            jnp.concatenate(
                [results[n][side] if n else jnp.zeros_like(results[0][side]) for n in order]
            )
        )
        grads.append(lax.dynamic_update_slice_in_dim(base, results[0][side], cuts[0][0], 0))
    key_grad, value_grad = grads
    return (query_out, key_grad, value_grad)


def solution(mesh):
    return jax.shard_map(
        body,
        mesh=mesh,
        in_specs=(
            P(None, ("blk", "ulysses"), None),
            P(None, ("blk", "ulysses"), None),
            P(None, "blk", None),
            P(None, "blk", None),
            P(),
        ),
        out_specs=(
            P(None, ("blk", "ulysses"), None),
            P(None, ("blk", "ulysses"), None),
            P(None, ("blk", "ulysses"), None),
        ),
        check_vma=False,
    )
```

```python
import functools
import math

import jax
import jax.numpy as jnp
from jax import lax
from jax.experimental import pallas as pl
from jax.experimental.pallas import tpu as pltpu
from jax.sharding import PartitionSpec as P


KB = 16
PLAN = ((16, 16, False, (1, 2)), (0, 16, True, (2,)))
STEP_HEADS = 8
VMEM_SMALL = 8 << 20
VMEM_ATTEND = 16 << 20


def far_masks(groups):
    return list(range(1, groups))


def pick_kernel(cuts, groups, routes, query, grad, keys, values, *rest):
    outs, arrived = list(rest[:-1]), rest[-1]
    group = lax.axis_index("blk")
    half = lax.axis_index("ulysses") % 2
    copies = []
    for number, (first_head, heads, paired, _) in enumerate(cuts):
        if paired:
            heads //= 2
            other = first_head + (1 - half) * heads
            first_head = first_head + half * heads
            swapped = outs.pop(0)
            for side, rows in enumerate((query, grad)):
                copies.append(
                    pltpu.make_async_copy(
                        rows.at[pl.ds(other, heads)],
                        swapped.at[side],
                        arrived.at[number, groups - 1, side],
                    )
                )
        for index, mask in enumerate(far_masks(groups)):
            out = outs[index]
            start = pl.multiple_of(routes[group ^ mask, group] * KB, KB)
            for side, rows in enumerate((keys, values)):
                copies.append(
                    pltpu.make_async_copy(
                        rows.at[pl.ds(first_head, heads), pl.ds(start, KB)],
                        out.at[side],
                        arrived.at[number, index, side],
                    )
                )
        outs = outs[groups - 1 :]
    for copy in copies:
        copy.start()
    for copy in copies:
        copy.wait()


def pick(routes, query, grad, keys, values, groups, cuts):
    _, tokens, head_dim = query.shape
    shapes, counts = [], []
    for _, heads, paired, _ in cuts:
        heads = heads // 2 if paired else heads
        block = (2, heads, KB, head_dim)
        swap = [(2, heads, tokens, head_dim)] if paired else []
        shapes += swap + [block] * (groups - 1)
        counts.append(len(swap) + groups - 1)
    outs = pl.pallas_call(
        functools.partial(pick_kernel, cuts, groups),
        out_shape=[jax.ShapeDtypeStruct(shape, jnp.bfloat16) for shape in shapes],
        in_specs=[pl.BlockSpec(memory_space=pltpu.SMEM)]
        + [pl.BlockSpec(memory_space=pltpu.HBM)] * 4,
        out_specs=[pl.BlockSpec(memory_space=pltpu.VMEM)] * len(shapes),
        scratch_shapes=[pltpu.SemaphoreType.DMA((len(cuts), groups, 2))],
        compiler_params=pltpu.CompilerParams(vmem_limit_bytes=VMEM_SMALL),
        name="pick",
    )(routes, query, grad, keys, values)
    picked = []
    for count, cut in zip(counts, cuts):
        mine, outs = outs[:count], outs[count:]
        picked.append((mine[0], mine[1:]) if cut[2] else (None, mine))
    return picked


def slot_specs(groups, step_heads, rows, head_dim):
    spec = pl.BlockSpec(
        (2, step_heads) + rows + (head_dim,), lambda i, *_: (0, i) + (0,) * (len(rows) + 1)
    )
    return [spec] * (groups - 1)


def attend_kernel(masks, has_alias, paired, _, query, grad, keys, values, *rest):
    slots = len(masks)
    far_rows = rest[:slots]
    swapped = rest[slots] if paired else None
    rest = rest[slots + has_alias + paired :]
    if paired:
        other_out, rest = rest[0], rest[1:]
    query_out, own_out = rest[:2]
    far_outs = rest[2 : 2 + slots]
    score_ref, dweight_ref, half_ref, dscore_ref = rest[2 + slots :]
    heads, tokens, head_dim = query.shape
    group_keys = keys.shape[1]
    group = lax.axis_index("blk")
    rank = lax.axis_index("ulysses")
    key_stride = tokens * lax.axis_size("ulysses") // group_keys
    score_scale = 1.0 / math.sqrt(head_dim)
    exp_scale = score_scale * math.log2(math.e)
    key_at = lax.broadcasted_iota(jnp.int32, (group_keys, tokens), 0) * key_stride
    token_at = lax.broadcasted_iota(jnp.int32, (group_keys, tokens), 1)
    sources = (rank, rank ^ 1) if paired else (rank,)
    hidden = [
        jnp.concatenate(
            [jnp.where(key_at <= token_at + source * tokens, 0.0, -jnp.inf) for source in sources],
            axis=1,
        )
    ]
    for mask in masks:
        seen = jnp.where((group ^ mask) < group, 0.0, -jnp.inf)
        hidden.append(jnp.full((KB, tokens * len(sources)), seen, jnp.float32))
    hidden = jnp.concatenate(hidden, axis=0)
    nt = (((1,), (1,)), ((), ()))
    tn = (((0,), (0,)), ((), ()))

    def near(rows, side, head):
        return jnp.concatenate([rows[head]] + [far[side, head] for far in far_rows], axis=0)

    def both(rows, side, head):
        if not paired:
            return rows[head]
        return jnp.concatenate([rows[head], swapped[side, head]], axis=0)

    for head in range(heads):
        score_ref[head] = lax.dot_general(
            near(keys, 0, head), both(query, 0, head), nt, preferred_element_type=jnp.float32
        )
        dweight_ref[head] = lax.dot_general(
            near(values, 1, head), both(grad, 1, head), nt, preferred_element_type=jnp.float32
        )
    for head in range(heads):
        scores = score_ref[head] + hidden
        dweights = dweight_ref[head]
        row_max = jnp.max(scores, axis=0, keepdims=True)
        expsum = jnp.exp2((scores - row_max) * exp_scale)
        weights = expsum * (1.0 / jnp.sum(expsum, axis=0, keepdims=True))
        weights_half = weights.astype(jnp.bfloat16)
        delta = jnp.sum(weights_half.astype(jnp.float32) * dweights, axis=0, keepdims=True)
        half_ref[head] = weights_half
        dscore_ref[head] = (weights * (dweights - delta)).astype(jnp.bfloat16)
    for head in range(heads):
        dscore = dscore_ref[head]
        query_grad = lax.dot_general(
            dscore, near(keys, 0, head), tn, preferred_element_type=jnp.float32
        )
        query_grad = (query_grad * score_scale).astype(jnp.bfloat16)
        query_out[head] = query_grad[:tokens]
        if paired:
            other_out[head] = query_grad[tokens:]
        key_part = jnp.dot(dscore, both(query, 0, head), preferred_element_type=jnp.float32)
        value_part = jnp.dot(
            half_ref[head], both(grad, 1, head), preferred_element_type=jnp.float32
        )
        parts = ((key_part * score_scale).astype(jnp.bfloat16), value_part.astype(jnp.bfloat16))
        for side, part in enumerate(parts):
            own_out[side, head] = part[:group_keys]
            for slot, far_out in enumerate(far_outs):
                start = group_keys + slot * KB
                far_out[side, head] = part[start : start + KB]


def step_of(heads, *offsets):
    return max(step for step in range(1, STEP_HEADS + 1) if math.gcd(step, heads, *offsets) == step)


def attend(half, rows, far, swapped, groups, cut, query_shape, query_out):
    first_head, heads, paired, _ = cut
    _, tokens, head_dim = query_shape
    group_keys = rows[2].shape[1]
    masks = far_masks(groups)
    near_keys = group_keys + KB * len(masks)
    if paired:
        heads //= 2
    step_heads = step_of(heads, first_head)
    first_step = first_head // step_heads
    half_steps = heads // step_heads if paired else 0

    def placed(count):
        return pl.BlockSpec(
            (step_heads, count, head_dim),
            lambda i, half: (first_step + half[0] * half_steps + i, 0, 0),
        )

    def pair(count):
        return pl.BlockSpec((2, step_heads, count, head_dim), lambda i, half: (0, i, 0, 0))

    block = (2, heads, KB, head_dim)
    shapes = [query_shape, (2, heads, group_keys, head_dim)] + [block] * len(masks)
    out_specs = [placed(tokens), pair(group_keys)] + [pair(KB)] * len(masks)
    operands = [half, *rows, *far]
    in_specs = [placed(tokens)] * 2 + [placed(group_keys)] * 2
    in_specs += slot_specs(groups, step_heads, (KB,), head_dim)
    aliases = {}
    if paired:
        operands.append(swapped)
        in_specs.append(pair(tokens))
        shapes.insert(0, (heads, tokens, head_dim))
        out_specs.insert(
            0, pl.BlockSpec((step_heads, tokens, head_dim), lambda i, half: (i, 0, 0))
        )
    if query_out is not None:
        aliases = {len(operands): int(paired)}
        operands.append(query_out)
        in_specs.append(pl.BlockSpec(memory_space=pl.ANY))
    scores = (step_heads, near_keys, tokens * (1 + paired))
    outs = pl.pallas_call(
        functools.partial(attend_kernel, masks, query_out is not None, paired),
        out_shape=[jax.ShapeDtypeStruct(shape, jnp.bfloat16) for shape in shapes],
        grid_spec=pltpu.PrefetchScalarGridSpec(
            num_scalar_prefetch=1,
            grid=(heads // step_heads,),
            in_specs=in_specs,
            out_specs=out_specs,
            scratch_shapes=[pltpu.VMEM(scores, jnp.float32)] * 2
            + [pltpu.VMEM(scores, jnp.bfloat16)] * 2,
        ),
        input_output_aliases=aliases,
        compiler_params=pltpu.CompilerParams(vmem_limit_bytes=VMEM_ATTEND),
        name="attend",
    )(*operands)
    other = None
    if paired:
        other, outs = outs[0], outs[1:]
    return other, outs[0], outs[1], outs[2:]


def mixes(bits):
    found = [0]
    for bit in bits:
        found += [mask | bit for mask in found]
    return found


def merge_kernel(masks, bits, routes, own, *rest):
    slots = len(masks)
    back = rest[:slots]
    outs, total = rest[slots:-1], rest[-1]
    group = lax.axis_index("blk")
    rank = lax.axis_index("ulysses")
    per_block = back[0].shape[2]
    total[...] = own[...].astype(jnp.float32)
    for mask, part in zip(masks, back):
        first = routes[group ^ mask, group] * per_block
        spot = pl.ds(first, per_block)
        total[:, :, spot] = total[:, :, spot] + part[...].astype(jnp.float32)
    chosen = sum(bits)
    bases = [index for index in range(own.shape[2]) if index & chosen == 0]
    for mix, out in zip(mixes(bits), outs):
        for index, base in enumerate(bases):
            out[:, :, index] = total[:, :, base + ((rank ^ mix) & chosen)].astype(jnp.bfloat16)


def merge(routes, own, back, groups, ranks, bits):
    _, chunk_heads, group_keys, head_dim = own.shape
    rank_keys = group_keys // ranks
    step_heads = step_of(chunk_heads)
    masks = far_masks(groups)
    rows = (KB // rank_keys, rank_keys)

    def blocks(count):
        return pl.BlockSpec(
            (2, step_heads, count, rank_keys, head_dim), lambda i: (0, i, 0, 0, 0)
        )

    pieces = 1 << len(bits)
    piece = (2, chunk_heads, ranks // pieces, rank_keys, head_dim)
    return pl.pallas_call(
        functools.partial(merge_kernel, masks, bits),
        out_shape=[jax.ShapeDtypeStruct(piece, jnp.bfloat16)] * pieces,
        grid=(chunk_heads // step_heads,),
        in_specs=[pl.BlockSpec(memory_space=pltpu.SMEM), blocks(ranks)]
        + slot_specs(groups, step_heads, rows, head_dim),
        out_specs=[blocks(ranks // pieces)] * pieces,
        scratch_shapes=[
            pltpu.VMEM((2, step_heads, ranks, rank_keys, head_dim), jnp.float32)
        ],
        compiler_params=pltpu.CompilerParams(vmem_limit_bytes=VMEM_ATTEND),
        name="merge",
    )(
        routes,
        own.reshape(2, chunk_heads, ranks, rank_keys, head_dim),
        *(part.reshape(part.shape[:-2] + rows + (head_dim,)) for part in back),
    )


def body(query_rows, out_grad, key_rows, value_rows, routes):
    head_count, _, head_dim = query_rows.shape
    query_rows, out_grad, key_rows, value_rows, routes = (
        pltpu.with_memory_space_constraint(rows, pltpu.HBM)
        for rows in (query_rows, out_grad, key_rows, value_rows, routes)
    )
    group_keys = key_rows.shape[1]
    groups = lax.axis_size("blk")
    ranks = lax.axis_size("ulysses")
    my_rank = lax.axis_index("ulysses")
    rank_keys = group_keys // ranks
    half = my_rank % 2
    bits = [1 << b for b in range(ranks.bit_length() - 1)]
    whole = sum(parts for _, parts, _, _ in PLAN)
    cuts = [
        (head_count * first // whole, head_count * parts // whole, paired, order)
        for first, parts, paired, order in PLAN
    ]

    def exchange(parts):
        came = []
        for mask, part in zip(far_masks(groups), parts):
            came.append(lax.ppermute(part, "blk", [(g, g ^ mask) for g in range(groups)]))
        return came

    def scatter(pieces, stages):
        left = [bit for bit in bits]
        for step, stage in enumerate(stages):
            left = [bit for bit in left if bit not in stage]
            shape = (2, pieces[0].shape[1]) + (2,) * len(left) + (rank_keys, head_dim)
            came = []
            for mix, piece in zip(mixes(stage)[1:], pieces[1:]):
                came.append(
                    lax.ppermute(
                        piece.reshape(shape), "ulysses", [(r, r ^ mix) for r in range(ranks)]
                    )
                )
            total = pieces[0].reshape(shape).astype(jnp.float32)
            for part in came:
                total = total + part.astype(jnp.float32)
            if step + 1 == len(stages):
                return total
            total = total.astype(jnp.bfloat16)
            after = stages[step + 1]
            rest = [bit for bit in left if bit not in after]
            axes = [2 + sum(b > bit for b in rest + list(after)) for bit in after]
            pieces = []
            for mix in mixes(after):
                starts = [0] * total.ndim
                sizes = list(total.shape)
                for bit, axis in zip(after, axes):
                    starts[axis] = ((my_rank ^ mix) // bit) % 2
                    sizes[axis] = 1
                pieces.append(lax.dynamic_slice(total, starts, sizes))

    def trade(rows):
        return lax.ppermute(rows, "ulysses", [(r, r ^ 1) for r in range(ranks)])

    def join(total):
        mine = lax.dynamic_index_in_dim(total, half, 2, keepdims=False)
        away = lax.dynamic_index_in_dim(total, 1 - half, 2, keepdims=False)
        came = trade(away.astype(jnp.bfloat16)).astype(jnp.float32)
        low = jnp.where(half == 0, mine, came)
        high = jnp.where(half == 0, came, mine)
        return jnp.concatenate([low, high], axis=1)

    half_operand = half.astype(jnp.int32).reshape(1)
    picked = pick(routes, query_rows, out_grad, key_rows, value_rows, groups, cuts)
    local_rows = (query_rows, out_grad, key_rows, value_rows)
    query_out = None
    results = []
    others = []
    fetched = []
    for swapped, parts in picked:
        if swapped is not None:
            swapped = trade(swapped)
        fetched.append((swapped, exchange(parts)))
    for number, cut in enumerate(cuts):
        swapped, far = fetched[number]
        other, query_out, own, parts = attend(
            half_operand, local_rows, far, swapped, groups, cut, query_rows.shape, query_out
        )
        back = exchange(parts)
        if other is not None:
            others.append((cut, trade(other)))
        wanted = [bit for bit in bits if not (cut[2] and bit == 1)]
        stages = []
        for size in cut[3] + (1,) * len(bits):
            if wanted:
                stages.append(tuple(wanted[:size]))
                wanted = wanted[size:]
        pieces = merge(routes, own, back, groups, ranks, stages[0])
        total = scatter(pieces, stages)
        if cut[2]:
            total = join(total)
        results.append(total)
    for cut, rows in others:
        first = cut[0] + (1 - half) * (cut[1] // 2)
        query_out = lax.dynamic_update_slice_in_dim(query_out, rows, first, 0)
    order = sorted(range(len(cuts)), key=lambda number: cuts[number][0])
    grads = []
    for side in range(2):
        base = lax.optimization_barrier(
            jnp.concatenate(
                [results[n][side] if n else jnp.zeros_like(results[0][side]) for n in order]
            )
        )
        grads.append(lax.dynamic_update_slice_in_dim(base, results[0][side], cuts[0][0], 0))
    key_grad, value_grad = grads
    return (query_out, key_grad, value_grad)


def solution(mesh):
    return jax.shard_map(
        body,
        mesh=mesh,
        in_specs=(
            P(None, ("blk", "ulysses"), None),
            P(None, ("blk", "ulysses"), None),
            P(None, "blk", None),
            P(None, "blk", None),
            P(),
        ),
        out_specs=(
            P(None, ("blk", "ulysses"), None),
            P(None, ("blk", "ulysses"), None),
            P(None, ("blk", "ulysses"), None),
        ),
        check_vma=False,
    )
```

```python
import functools
import math

import jax
import jax.numpy as jnp
from jax import lax
from jax.experimental import pallas as pl
from jax.experimental.pallas import tpu as pltpu
from jax.sharding import PartitionSpec as P


KB = 16
PLAN = ((16, 16, False, ((1, 2), (1, 1, 1))), (0, 16, True, (2,)))
STEP_HEADS = 8
VMEM_SMALL = 8 << 20
VMEM_ATTEND = 16 << 20


def far_masks(groups):
    return list(range(1, groups))


def pick_kernel(cuts, groups, routes, query, grad, keys, values, *rest):
    outs, arrived = list(rest[:-1]), rest[-1]
    group = lax.axis_index("blk")
    half = lax.axis_index("ulysses") % 2
    copies = []
    for number, (first_head, heads, paired, _) in enumerate(cuts):
        if paired:
            heads //= 2
            other = first_head + (1 - half) * heads
            first_head = first_head + half * heads
            swapped = outs.pop(0)
            for side, rows in enumerate((query, grad)):
                copies.append(
                    pltpu.make_async_copy(
                        rows.at[pl.ds(other, heads)],
                        swapped.at[side],
                        arrived.at[number, groups - 1, side],
                    )
                )
        for index, mask in enumerate(far_masks(groups)):
            out = outs[index]
            start = pl.multiple_of(routes[group ^ mask, group] * KB, KB)
            for side, rows in enumerate((keys, values)):
                copies.append(
                    pltpu.make_async_copy(
                        rows.at[pl.ds(first_head, heads), pl.ds(start, KB)],
                        out.at[side],
                        arrived.at[number, index, side],
                    )
                )
        outs = outs[groups - 1 :]
    for copy in copies:
        copy.start()
    for copy in copies:
        copy.wait()


def pick(routes, query, grad, keys, values, groups, cuts):
    _, tokens, head_dim = query.shape
    shapes, counts = [], []
    for _, heads, paired, _ in cuts:
        heads = heads // 2 if paired else heads
        block = (2, heads, KB, head_dim)
        swap = [(2, heads, tokens, head_dim)] if paired else []
        shapes += swap + [block] * (groups - 1)
        counts.append(len(swap) + groups - 1)
    outs = pl.pallas_call(
        functools.partial(pick_kernel, cuts, groups),
        out_shape=[jax.ShapeDtypeStruct(shape, jnp.bfloat16) for shape in shapes],
        in_specs=[pl.BlockSpec(memory_space=pltpu.SMEM)]
        + [pl.BlockSpec(memory_space=pltpu.HBM)] * 4,
        out_specs=[pl.BlockSpec(memory_space=pltpu.VMEM)] * len(shapes),
        scratch_shapes=[pltpu.SemaphoreType.DMA((len(cuts), groups, 2))],
        compiler_params=pltpu.CompilerParams(vmem_limit_bytes=VMEM_SMALL),
        name="pick",
    )(routes, query, grad, keys, values)
    picked = []
    for count, cut in zip(counts, cuts):
        mine, outs = outs[:count], outs[count:]
        picked.append((mine[0], mine[1:]) if cut[2] else (None, mine))
    return picked


def slot_specs(groups, step_heads, rows, head_dim):
    spec = pl.BlockSpec(
        (2, step_heads) + rows + (head_dim,), lambda i, *_: (0, i) + (0,) * (len(rows) + 1)
    )
    return [spec] * (groups - 1)


def attend_kernel(masks, has_alias, paired, _, query, grad, keys, values, *rest):
    slots = len(masks)
    far_rows = rest[:slots]
    swapped = rest[slots] if paired else None
    rest = rest[slots + has_alias + paired :]
    if paired:
        other_out, rest = rest[0], rest[1:]
    query_out, own_out = rest[:2]
    far_outs = rest[2 : 2 + slots]
    score_ref, dweight_ref, half_ref, dscore_ref = rest[2 + slots :]
    heads, tokens, head_dim = query.shape
    group_keys = keys.shape[1]
    group = lax.axis_index("blk")
    rank = lax.axis_index("ulysses")
    key_stride = tokens * lax.axis_size("ulysses") // group_keys
    score_scale = 1.0 / math.sqrt(head_dim)
    exp_scale = score_scale * math.log2(math.e)
    key_at = lax.broadcasted_iota(jnp.int32, (group_keys, tokens), 0) * key_stride
    token_at = lax.broadcasted_iota(jnp.int32, (group_keys, tokens), 1)
    sources = (rank, rank ^ 1) if paired else (rank,)
    hidden = [
        jnp.concatenate(
            [jnp.where(key_at <= token_at + source * tokens, 0.0, -jnp.inf) for source in sources],
            axis=1,
        )
    ]
    for mask in masks:
        seen = jnp.where((group ^ mask) < group, 0.0, -jnp.inf)
        hidden.append(jnp.full((KB, tokens * len(sources)), seen, jnp.float32))
    hidden = jnp.concatenate(hidden, axis=0)
    nt = (((1,), (1,)), ((), ()))
    tn = (((0,), (0,)), ((), ()))

    def near(rows, side, head):
        return jnp.concatenate([rows[head]] + [far[side, head] for far in far_rows], axis=0)

    def both(rows, side, head):
        if not paired:
            return rows[head]
        return jnp.concatenate([rows[head], swapped[side, head]], axis=0)

    for head in range(heads):
        score_ref[head] = lax.dot_general(
            near(keys, 0, head), both(query, 0, head), nt, preferred_element_type=jnp.float32
        )
        dweight_ref[head] = lax.dot_general(
            near(values, 1, head), both(grad, 1, head), nt, preferred_element_type=jnp.float32
        )
    for head in range(heads):
        scores = score_ref[head] + hidden
        dweights = dweight_ref[head]
        row_max = jnp.max(scores, axis=0, keepdims=True)
        expsum = jnp.exp2((scores - row_max) * exp_scale)
        weights = expsum * (1.0 / jnp.sum(expsum, axis=0, keepdims=True))
        weights_half = weights.astype(jnp.bfloat16)
        delta = jnp.sum(weights_half.astype(jnp.float32) * dweights, axis=0, keepdims=True)
        half_ref[head] = weights_half
        dscore_ref[head] = (weights * (dweights - delta)).astype(jnp.bfloat16)
    for head in range(heads):
        dscore = dscore_ref[head]
        query_grad = lax.dot_general(
            dscore, near(keys, 0, head), tn, preferred_element_type=jnp.float32
        )
        query_grad = (query_grad * score_scale).astype(jnp.bfloat16)
        query_out[head] = query_grad[:tokens]
        if paired:
            other_out[head] = query_grad[tokens:]
        key_part = jnp.dot(dscore, both(query, 0, head), preferred_element_type=jnp.float32)
        value_part = jnp.dot(
            half_ref[head], both(grad, 1, head), preferred_element_type=jnp.float32
        )
        parts = ((key_part * score_scale).astype(jnp.bfloat16), value_part.astype(jnp.bfloat16))
        for side, part in enumerate(parts):
            own_out[side, head] = part[:group_keys]
            for slot, far_out in enumerate(far_outs):
                start = group_keys + slot * KB
                far_out[side, head] = part[start : start + KB]


def step_of(heads, *offsets):
    return max(step for step in range(1, STEP_HEADS + 1) if math.gcd(step, heads, *offsets) == step)


def attend(half, rows, far, swapped, groups, cut, query_shape, query_out):
    first_head, heads, paired, _ = cut
    _, tokens, head_dim = query_shape
    group_keys = rows[2].shape[1]
    masks = far_masks(groups)
    near_keys = group_keys + KB * len(masks)
    if paired:
        heads //= 2
    step_heads = step_of(heads, first_head)
    first_step = first_head // step_heads
    half_steps = heads // step_heads if paired else 0

    def placed(count):
        return pl.BlockSpec(
            (step_heads, count, head_dim),
            lambda i, half: (first_step + half[0] * half_steps + i, 0, 0),
        )

    def pair(count):
        return pl.BlockSpec((2, step_heads, count, head_dim), lambda i, half: (0, i, 0, 0))

    block = (2, heads, KB, head_dim)
    shapes = [query_shape, (2, heads, group_keys, head_dim)] + [block] * len(masks)
    out_specs = [placed(tokens), pair(group_keys)] + [pair(KB)] * len(masks)
    operands = [half, *rows, *far]
    in_specs = [placed(tokens)] * 2 + [placed(group_keys)] * 2
    in_specs += slot_specs(groups, step_heads, (KB,), head_dim)
    aliases = {}
    if paired:
        operands.append(swapped)
        in_specs.append(pair(tokens))
        shapes.insert(0, (heads, tokens, head_dim))
        out_specs.insert(
            0, pl.BlockSpec((step_heads, tokens, head_dim), lambda i, half: (i, 0, 0))
        )
    if query_out is not None:
        aliases = {len(operands): int(paired)}
        operands.append(query_out)
        in_specs.append(pl.BlockSpec(memory_space=pl.ANY))
    scores = (step_heads, near_keys, tokens * (1 + paired))
    outs = pl.pallas_call(
        functools.partial(attend_kernel, masks, query_out is not None, paired),
        out_shape=[jax.ShapeDtypeStruct(shape, jnp.bfloat16) for shape in shapes],
        grid_spec=pltpu.PrefetchScalarGridSpec(
            num_scalar_prefetch=1,
            grid=(heads // step_heads,),
            in_specs=in_specs,
            out_specs=out_specs,
            scratch_shapes=[pltpu.VMEM(scores, jnp.float32)] * 2
            + [pltpu.VMEM(scores, jnp.bfloat16)] * 2,
        ),
        input_output_aliases=aliases,
        compiler_params=pltpu.CompilerParams(vmem_limit_bytes=VMEM_ATTEND),
        name="attend",
    )(*operands)
    other = None
    if paired:
        other, outs = outs[0], outs[1:]
    return other, outs[0], outs[1], outs[2:]


def mixes(bits):
    found = [0]
    for bit in bits:
        found += [mask | bit for mask in found]
    return found


def merge_kernel(masks, firsts, routes, own, *rest):
    slots = len(masks)
    back = rest[:slots]
    outs, total = rest[slots:-1], rest[-1]
    group = lax.axis_index("blk")
    rank = lax.axis_index("ulysses")
    per_block = back[0].shape[2]
    total[...] = own[...].astype(jnp.float32)
    for mask, part in zip(masks, back):
        first = routes[group ^ mask, group] * per_block
        spot = pl.ds(first, per_block)
        total[:, :, spot] = total[:, :, spot] + part[...].astype(jnp.float32)
    outs = list(outs)
    for side, bits in enumerate(firsts):
        sides = slice(side, side + 1) if len(firsts) > 1 else slice(0, 2)
        chosen = sum(bits)
        bases = [index for index in range(own.shape[2]) if index & chosen == 0]
        for mix in mixes(bits):
            out = outs.pop(0)
            for index, base in enumerate(bases):
                spot = base + ((rank ^ mix) & chosen)
                out[:, :, index] = total[sides, :, spot].astype(jnp.bfloat16)


def merge(routes, own, back, groups, ranks, firsts):
    _, chunk_heads, group_keys, head_dim = own.shape
    rank_keys = group_keys // ranks
    step_heads = math.gcd(16, chunk_heads)
    masks = far_masks(groups)
    rows = (KB // rank_keys, rank_keys)

    def blocks(sides, count):
        return pl.BlockSpec(
            (sides, step_heads, count, rank_keys, head_dim), lambda i: (0, i, 0, 0, 0)
        )

    sides = 2 // len(firsts)
    counts = [ranks >> len(bits) for bits in firsts for _ in mixes(bits)]
    outs = pl.pallas_call(
        functools.partial(merge_kernel, masks, firsts),
        out_shape=[
            jax.ShapeDtypeStruct((sides, chunk_heads, count, rank_keys, head_dim), jnp.bfloat16)
            for count in counts
        ],
        grid=(chunk_heads // step_heads,),
        in_specs=[pl.BlockSpec(memory_space=pltpu.SMEM), blocks(2, ranks)]
        + slot_specs(groups, step_heads, rows, head_dim),
        out_specs=[blocks(sides, count) for count in counts],
        scratch_shapes=[
            pltpu.VMEM((2, step_heads, ranks, rank_keys, head_dim), jnp.float32)
        ],
        compiler_params=pltpu.CompilerParams(vmem_limit_bytes=VMEM_ATTEND),
        name="merge",
    )(
        routes,
        own.reshape(2, chunk_heads, ranks, rank_keys, head_dim),
        *(part.reshape(part.shape[:-2] + rows + (head_dim,)) for part in back),
    )
    pieces = []
    for bits in firsts:
        pieces.append(outs[: 1 << len(bits)])
        outs = outs[1 << len(bits) :]
    return pieces


def body(query_rows, out_grad, key_rows, value_rows, routes):
    head_count, _, head_dim = query_rows.shape
    query_rows, out_grad, key_rows, value_rows, routes = (
        pltpu.with_memory_space_constraint(rows, pltpu.HBM)
        for rows in (query_rows, out_grad, key_rows, value_rows, routes)
    )
    group_keys = key_rows.shape[1]
    groups = lax.axis_size("blk")
    ranks = lax.axis_size("ulysses")
    my_rank = lax.axis_index("ulysses")
    rank_keys = group_keys // ranks
    half = my_rank % 2
    bits = [1 << b for b in range(ranks.bit_length() - 1)]
    whole = sum(parts for _, parts, _, _ in PLAN)
    cuts = [
        (head_count * first // whole, head_count * parts // whole, paired, order)
        for first, parts, paired, order in PLAN
    ]

    def exchange(parts):
        came = []
        for mask, part in zip(far_masks(groups), parts):
            came.append(lax.ppermute(part, "blk", [(g, g ^ mask) for g in range(groups)]))
        return came

    def scatter(pieces, stages):
        left = [bit for bit in bits]
        for step, stage in enumerate(stages):
            left = [bit for bit in left if bit not in stage]
            shape = pieces[0].shape[:2] + (2,) * len(left) + (rank_keys, head_dim)
            came = []
            for mix, piece in zip(mixes(stage)[1:], pieces[1:]):
                came.append(
                    lax.ppermute(
                        piece.reshape(shape), "ulysses", [(r, r ^ mix) for r in range(ranks)]
                    )
                )
            total = pieces[0].reshape(shape).astype(jnp.float32)
            for part in came:
                total = total + part.astype(jnp.float32)
            if step + 1 == len(stages):
                return total
            total = total.astype(jnp.bfloat16)
            after = stages[step + 1]
            rest = [bit for bit in left if bit not in after]
            axes = [2 + sum(b > bit for b in rest + list(after)) for bit in after]
            pieces = []
            for mix in mixes(after):
                starts = [0] * total.ndim
                sizes = list(total.shape)
                for bit, axis in zip(after, axes):
                    starts[axis] = ((my_rank ^ mix) // bit) % 2
                    sizes[axis] = 1
                pieces.append(lax.dynamic_slice(total, starts, sizes))

    def trade(rows):
        return lax.ppermute(rows, "ulysses", [(r, r ^ 1) for r in range(ranks)])

    def join(total):
        mine = lax.dynamic_index_in_dim(total, half, 2, keepdims=False)
        away = lax.dynamic_index_in_dim(total, 1 - half, 2, keepdims=False)
        came = trade(away.astype(jnp.bfloat16)).astype(jnp.float32)
        low = jnp.where(half == 0, mine, came)
        high = jnp.where(half == 0, came, mine)
        return jnp.concatenate([low, high], axis=1)

    half_operand = half.astype(jnp.int32).reshape(1)
    picked = pick(routes, query_rows, out_grad, key_rows, value_rows, groups, cuts)
    local_rows = (query_rows, out_grad, key_rows, value_rows)
    query_out = None
    results = []
    others = []
    fetched = []
    for swapped, parts in picked:
        if swapped is not None:
            swapped = trade(swapped)
        fetched.append((swapped, exchange(parts)))
    for number, cut in enumerate(cuts):
        swapped, far = fetched[number]
        other, query_out, own, parts = attend(
            half_operand, local_rows, far, swapped, groups, cut, query_rows.shape, query_out
        )
        back = exchange(parts)
        if other is not None:
            others.append((cut, trade(other)))
        split = isinstance(cut[3][0], tuple)
        plans = []
        for sizes in cut[3] if split else (cut[3],):
            wanted = [bit for bit in bits if not (cut[2] and bit == 1)]
            plans.append([])
            for size in sizes + (1,) * len(bits):
                if wanted:
                    plans[-1].append(tuple(wanted[:size]))
                    wanted = wanted[size:]
        pieces = merge(routes, own, back, groups, ranks, [stages[0] for stages in plans])
        total = [scatter(pieces[i], stages) for i, stages in enumerate(plans)]
        if split:
            total = jnp.concatenate(total, axis=0) if cut[2] else [part[0] for part in total]
        else:
            total = total[0]
        if cut[2]:
            total = join(total)
        results.append(total)
    for cut, rows in others:
        first = cut[0] + (1 - half) * (cut[1] // 2)
        query_out = lax.dynamic_update_slice_in_dim(query_out, rows, first, 0)
    order = sorted(range(len(cuts)), key=lambda number: cuts[number][0])
    grads = []
    for side in range(2):
        base = lax.optimization_barrier(
            jnp.concatenate(
                [results[n][side] if n else jnp.zeros_like(results[0][side]) for n in order]
            )
        )
        grads.append(lax.dynamic_update_slice_in_dim(base, results[0][side], cuts[0][0], 0))
    key_grad, value_grad = grads
    return (query_out, key_grad, value_grad)


def solution(mesh):
    return jax.shard_map(
        body,
        mesh=mesh,
        in_specs=(
            P(None, ("blk", "ulysses"), None),
            P(None, ("blk", "ulysses"), None),
            P(None, "blk", None),
            P(None, "blk", None),
            P(),
        ),
        out_specs=(
            P(None, ("blk", "ulysses"), None),
            P(None, ("blk", "ulysses"), None),
            P(None, ("blk", "ulysses"), None),
        ),
        check_vma=False,
    )
```
